32 devices in a mesh: row: 8 (over z, x), col: 4 (over y, core).
Axes of the slice: x: 2, y: 2, z: 4, core: 2. Of those that a mesh axis runs over, the one named last changes fastest.
Arguments:
- features: bfloat16 [8192, 256], P(('row', 'col')), may hold values from -6 to 6
- grad_out: bfloat16 [8192, 256], P(('row', 'col')), may hold values from -6 to 6
- degrees: int32 [8192], P(('row', 'col')), may hold values from 1 to 8236, as said below
- w_self: bfloat16 [256, 256], replicated, may hold values from -0.375 to 0.375
- w_neigh: bfloat16 [256, 256], replicated, may hold values from -0.375 to 0.375
- bias: float32 [256], replicated, may hold values from -4 to 4
- tile_slots: int32 [8, 4, 88], P('row', 'col'), may hold values from 0 to 127, as said below
- tile_count: int32 [8, 4], P('row', 'col'), may hold values from 22 to 88, as said below
- tile_masks: int32 [8, 4, 88, 16, 128], P('row', 'col'), may hold values from 0 to 255
Outputs:
- layer_out: bfloat16 [8192, 256], P(('row', 'col'))
- grad_in: bfloat16 [8192, 256], P(('row', 'col'))
- grad_w_self: float32 [256, 256], replicated
- grad_w_neigh: float32 [256, 256], replicated
The draws below stay inside these ranges and needn't reach their ends.
Inputs may be any that keep to these rules, and one draw needn't show every extreme that they name: `tile_slots`: on each device the 88 slot numbers are distinct and rise; slot s names block row s % 8 of the device's row group and block column s // 8 of its panel. Only a device's first tile_count tiles are live; the others are ignored. Some device holds 88 live tiles. `degrees`: each node's degree is at least the number of ones in its row of A, and at least 1; some node has the largest degree.
All inputs are finite; a program needn't handle non-finite values.
Results may differ from the reference program's by a relative error of at most 0.014.
Values may be sent and summed in bfloat16 or wider, within the bound.
No kernel may reach another device: no remote copies, remote signals or barrier semaphores. Data moves between devices by JAX's collectives and lax.ppermute only.
A program may use at most 64 MiB of HBM per device.

```python
import jax
import jax.numpy as jnp
from jax import lax

F = 256
B = 128
R = 256
TPR = 11
WORDS = 16
RB = 8
CB = 16
TPD = 88
NODES = 8192
N_ROW = 8
N_COL = 4


def draw_tile_slots(key, part):
    device_keys = jax.random.split(key, N_ROW * N_COL)
    chosen = jax.vmap(lambda device_key: jax.random.permutation(device_key, RB * CB)[:TPD])(device_keys)
    return jnp.sort(chosen, axis=-1).astype(jnp.int32).reshape(N_ROW, N_COL, TPD)


def draw_tile_count(key, part):
    divisors = jax.random.randint(key, (N_ROW * N_COL,), 1, 5, dtype=jnp.int32)
    counts = TPD // divisors
    busiest = jax.random.randint(jax.random.fold_in(key, 7), (), 0, N_ROW * N_COL, dtype=jnp.int32)
    counts = counts.at[busiest].set(TPD)
    return counts.astype(jnp.int32).reshape(N_ROW, N_COL)


def mask_parts(key):
    device_keys = jax.random.split(jax.random.fold_in(key, 11), N_ROW * N_COL)
    powers = jnp.left_shift(jnp.ones((8,), jnp.int32), jnp.arange(8, dtype=jnp.int32))

    def one_device(device_key):
        draws = jax.random.randint(device_key, (TPD, WORDS, 8, B), 0, 64, dtype=jnp.int32)
        bits = (draws == 0).astype(jnp.int32)
        words = jnp.sum(bits * powers[None, None, :, None], axis=2).astype(jnp.int32)
        row_ones = jnp.sum(bits, axis=(1, 2)).astype(jnp.int32)
        return (words, row_ones)
    words, row_ones = lax.map(one_device, device_keys)
    return (words, row_ones)


def draw_tile_masks(key, part):
    words, _ = mask_parts(key)
    return words.reshape(N_ROW, N_COL, TPD, WORDS, B).astype(jnp.int32)


def draw_degrees(key, part):
    device_count = N_ROW * N_COL
    slots = draw_tile_slots(key, part).reshape(device_count, TPD)
    counts = draw_tile_count(key, part).reshape(device_count)
    _, row_ones = mask_parts(key)
    positions = jnp.arange(TPD, dtype=jnp.int32)
    live = (positions[None, :] < counts[:, None]).astype(jnp.int32)
    row_ones = row_ones * live[:, :, None]
    device_rows = (jnp.arange(device_count, dtype=jnp.int32) // N_COL)[:, None]
    block_index = (device_rows * RB + slots % RB).astype(jnp.int32)
    totals = jnp.zeros((N_ROW * RB, B), jnp.int32).at[block_index.reshape(-1)].add(row_ones.reshape(device_count * TPD, B))
    outside_most = max(1, N_COL * TPR * B // 128)
    outside = jax.random.randint(jax.random.fold_in(key, 13), (NODES,), 1, outside_most + 1, dtype=jnp.int32)
    result = (totals.reshape(NODES) + outside).astype(jnp.int32)
    largest = N_COL * min(TPD, CB) * B + outside_most
    chosen_node = jax.random.randint(jax.random.fold_in(key, 17), (), 0, NODES, dtype=jnp.int32)
    result = result.at[chosen_node].set(jnp.int32(largest))
    return result.astype(jnp.int32)


def block_scale(own_key, shape, cuts, least, high):
    factor_of, own = 1.0, jax.random.fold_in(own_key, 6)
    for position, blocks in cuts:
        steps = jnp.exp(jax.random.uniform(jax.random.fold_in(own, position), (blocks,), jnp.float32, least / len(cuts), high / len(cuts)))
        factor_of = factor_of * jnp.repeat(steps, shape[position] // blocks).reshape([-1 if axis == position else 1 for axis in range(len(shape))])
    return factor_of


def noise(stream_key, shape, width, bound, shards=(), kind=jnp.bfloat16):
    values = jax.random.normal(stream_key, shape, jnp.float32) * width
    if len(shards) > 0:
        values = block_scale(stream_key, shape, shards, -0.22, 0.18) * values
    return jnp.clip(values, min=-bound, max=bound).astype(kind)


def setup_inputs(seed: int = 0) -> dict:
    key_list = jax.random.split(jax.random.key(seed), 10)
    features = noise(key_list[0], (NODES, F), 1.0, 6.0, ((0, 32),))
    grad_out = noise(key_list[1], (NODES, F), 1.0, 6.0, ((0, 32),))
    degrees = draw_degrees(jax.random.fold_in(key_list[9], 71), 0)
    w_self = noise(key_list[3], (F, F), F ** -0.5, 0.375)
    w_neigh = noise(key_list[4], (F, F), F ** -0.5, 0.375)
    bias = noise(key_list[5], (F,), 1.0, 4.0, (), jnp.float32)
    tile_slots = draw_tile_slots(jax.random.fold_in(key_list[9], 71), 0)
    tile_count = draw_tile_count(jax.random.fold_in(key_list[9], 71), 0)
    tile_masks = draw_tile_masks(jax.random.fold_in(key_list[9], 71), 0)
    return {"features": features, "grad_out": grad_out, "degrees": degrees, "w_self": w_self, "w_neigh": w_neigh, "bias": bias, "tile_slots": tile_slots, "tile_count": tile_count, "tile_masks": tile_masks}


def unpack_tiles(mask_words):
    shifts = jnp.arange(8, dtype=jnp.int32)
    bit_values = jnp.bitwise_and(jnp.right_shift(mask_words[:, :, None, :], shifts[None, None, :, None]), 1)
    return bit_values.reshape(mask_words.shape[0], mask_words.shape[1] * 8, mask_words.shape[2])


def reference(features, grad_out, degrees, w_self, w_neigh, bias, tile_slots, tile_count, tile_masks):
    device_count = N_ROW * N_COL
    slot_table = tile_slots.reshape(device_count, TPD)
    count_table = tile_count.reshape(device_count)
    mask_table = tile_masks.reshape(device_count, TPD, WORDS, B)
    positions = jnp.arange(TPD, dtype=jnp.int32)
    panels = features.reshape(N_ROW, N_COL, R, F)
    device_ids = jnp.arange(device_count, dtype=jnp.int32)

    def device_tiles(device):
        slot_ids = slot_table[device]
        is_live = (positions < count_table[device]).astype(jnp.float32)
        tile_bits = unpack_tiles(mask_table[device]).astype(jnp.float32) * is_live[:, None, None]
        return tile_bits, slot_ids % RB, slot_ids // RB

    def forward_step(summed, device):
        row_index = device // N_COL
        col_index = device % N_COL
        tile_bits, row_block, column_block = device_tiles(device)
        panel = lax.dynamic_index_in_dim(panels, col_index, axis=1, keepdims=False).reshape(CB, B, F)
        sources = panel[column_block].astype(jnp.float32)
        products = jnp.einsum("tji,tjf->tif", tile_bits, sources, precision=lax.Precision.HIGHEST)
        partial_value = jnp.zeros((RB, B, F), jnp.float32).at[row_block].add(products)
        partial_value = lax.optimization_barrier(partial_value.astype(jnp.bfloat16)).astype(jnp.float32)
        return summed.at[row_index].add(partial_value.reshape(RB * B, F)), None

    summed, _ = lax.scan(forward_step, jnp.zeros((N_ROW, RB * B, F), jnp.float32), device_ids)
    summed = summed.reshape(NODES, F)
    scale_degree = degrees.astype(jnp.float32)[:, None]
    mean_rows = (summed / scale_degree).astype(jnp.bfloat16)
    preact = jnp.dot(features, w_self, preferred_element_type=jnp.float32)
    preact = preact + jnp.dot(mean_rows, w_neigh, preferred_element_type=jnp.float32) + bias
    sigmoid_values = jax.nn.sigmoid(preact)
    layer_out = (preact * sigmoid_values).astype(jnp.bfloat16)
    grad_preact = (grad_out.astype(jnp.float32) * sigmoid_values * (1.0 + preact * (1.0 - sigmoid_values))).astype(jnp.bfloat16)
    grad_scale = NODES ** -0.5
    grad_w_self = jnp.dot(features.T, grad_preact, preferred_element_type=jnp.float32) * grad_scale
    grad_w_neigh = jnp.dot(mean_rows.T, grad_preact, preferred_element_type=jnp.float32) * grad_scale
    upward = (jnp.dot(grad_preact, w_neigh.T, preferred_element_type=jnp.float32) / scale_degree).astype(jnp.bfloat16)
    upward_groups = upward.reshape(N_ROW, RB, B, F)

    def backward_step(spread, device):
        row_index = device // N_COL
        col_index = device % N_COL
        tile_bits, row_block, column_block = device_tiles(device)
        group_rows = lax.dynamic_index_in_dim(upward_groups, row_index, axis=0, keepdims=False)
        sources = group_rows[row_block].astype(jnp.float32)
        products = jnp.einsum("tji,tif->tjf", tile_bits, sources, precision=lax.Precision.HIGHEST)
        partial_value = jnp.zeros((CB, B, F), jnp.float32).at[column_block].add(products)
        partial_value = lax.optimization_barrier(partial_value.astype(jnp.bfloat16)).astype(jnp.float32)
        return spread.at[col_index].add(partial_value.reshape(N_ROW, R, F)), None

    spread, _ = lax.scan(backward_step, jnp.zeros((N_COL, N_ROW, R, F), jnp.float32), device_ids)
    neighbor_grad = jnp.transpose(spread, (1, 0, 2, 3)).reshape(NODES, F)
    grad_in = (jnp.dot(grad_preact, w_self.T, preferred_element_type=jnp.float32) + neighbor_grad).astype(jnp.bfloat16)
    return layer_out, grad_in, grad_w_self, grad_w_neigh
```

```python
import functools
import math

import jax
import jax.numpy as jnp
from jax import lax
from jax.experimental import pallas as pl
from jax.experimental.pallas import tpu as pltpu
from jax.sharding import PartitionSpec as P


BOTH_FORMS_BYTES = 8 * 1024 * 1024

VMEM = pl.BlockSpec(memory_space=pltpu.VMEM)
SMEM = pl.BlockSpec(memory_space=pltpu.SMEM)

f32 = jnp.float32
bf16 = jnp.bfloat16


def mm(a, b):
    return jnp.dot(a, b, preferred_element_type=f32)


def mm_nt(a, b):
    return lax.dot_general(a, b, (((1,), (1,)), ((), ())), preferred_element_type=f32)


def mm_tn(a, b):
    return lax.dot_general(a, b, (((0,), (0,)), ((), ())), preferred_element_type=f32)


def params(*arrays):
    held = sum(math.prod(array.shape) * jnp.dtype(array.dtype).itemsize for array in arrays)
    return pltpu.CompilerParams(vmem_limit_bytes=held + held // 8 + (4 << 20))


def span(index, size):
    return pl.ds(pl.multiple_of(index * size, size), size)


def unpack_kernel(block_rows, slots_ref, count_ref, masks_ref, spread_ref, gather_ref=None):
    words, width = masks_ref.shape[1:]
    panel, group = spread_ref.shape

    @pl.loop(0, panel // width)
    def _(step):
        spread_ref[span(step, width), :] = jnp.zeros((width, group), bf16)

    if gather_ref is not None:

        @pl.loop(0, group // width)
        def _(step):
            gather_ref[span(step, width), :] = jnp.zeros((width, panel), bf16)

    shifts = lax.broadcasted_iota(jnp.int32, (words, 8, width), 1)

    @pl.loop(0, count_ref[0])
    def _(tile):
        slot = slots_ref[tile]
        row_block = lax.rem(slot, block_rows)
        column_block = lax.div(slot, block_rows)
        word = masks_ref[tile]
        spread_words = jnp.broadcast_to(word[:, None, :], (words, 8, width))
        bits = jnp.bitwise_and(jnp.right_shift(spread_words, shifts), 1)
        bits = bits.astype(f32).reshape(words * 8, width)
        spread_ref[span(column_block, width), span(row_block, width)] = bits.astype(bf16)
        if gather_ref is not None:
            gather_ref[span(row_block, width), span(column_block, width)] = bits.T.astype(bf16)


def unpack(slot_ids, live_count, masks, panel, group):
    both = 2 * panel * group * 2 <= BOTH_FORMS_BYTES
    shapes = [jax.ShapeDtypeStruct((panel, group), bf16)]
    if both:
        shapes.append(jax.ShapeDtypeStruct((group, panel), bf16))
    block_rows = group // masks.shape[2]
    return pl.pallas_call(
        functools.partial(unpack_kernel, block_rows),
        out_shape=shapes,
        in_specs=[SMEM, SMEM, VMEM],
        out_specs=[VMEM] * len(shapes),
        compiler_params=params(masks, *shapes),
        name="unpack",
    )(slot_ids, live_count, masks)


def forward_kernel(n_row, n_col, natural, place_ref, adjacency_ref, *refs):
    blocks, outs, panel_ref = refs[:n_row], refs[n_row : n_row + 2], refs[n_row + 2]
    rows = blocks[0].shape[0]
    row, col = place_ref[0], place_ref[1]
    for d in range(n_row):
        panel_ref[span(jnp.bitwise_xor(row, d), rows), :] = blocks[d][...]
    for e in list(range(1, n_col, 2)) + list(range(0, n_col, 2)):
        where = span(jnp.bitwise_xor(col, e), rows)
        if natural:
            total = mm(adjacency_ref[where, :], panel_ref[...])
        else:
            total = mm_tn(adjacency_ref[:, where], panel_ref[...])
        out = outs[e % 2]
        out[pl.ds((e // 2) * rows, rows), :] = total.astype(out.dtype)


def forward(place, adjacency, natural, blocks, n_col):
    rows, width = blocks[0].shape
    n_row = len(blocks)
    half = rows * n_col // 2
    shapes = [jax.ShapeDtypeStruct((half, width), kind) for kind in (f32, bf16)]
    return pl.pallas_call(
        functools.partial(forward_kernel, n_row, n_col, natural),
        out_shape=shapes,
        in_specs=[SMEM, VMEM] + [VMEM] * n_row,
        out_specs=[VMEM, VMEM],
        scratch_shapes=[pltpu.VMEM((rows * n_row, width), bf16)],
        compiler_params=params(adjacency, *blocks, *blocks, *shapes),
        name="forward",
    )(place, adjacency, *blocks)


def node_kernel(n_part, *refs):
    sums, refs = refs[:n_part], refs[n_part:]
    features, refs = refs[:n_part], refs[n_part:]
    cotangents, refs = refs[:n_part], refs[n_part:]
    degrees, refs = refs[:n_part], refs[n_part:]
    w_self, w_neigh, bias, out_ref, mean_ref, grad_ref, up_ref = refs
    rows = out_ref.shape[0]
    for h in range(n_part):
        parts = [sums[h2][pl.ds((h ^ h2) * rows, rows), :].astype(f32) for h2 in range(n_part)]
        while len(parts) > 1:
            parts = [parts[i] + parts[i + 1] for i in range(0, len(parts), 2)]
        inverse = 1.0 / degrees[h][...].astype(f32)
        mean = (parts[0] * inverse).astype(bf16)
        preact = mm(features[h][...], w_self[...]) + mm(mean, w_neigh[...]) + bias[...]
        gate = jax.nn.sigmoid(preact)
        if h == 0:
            out_ref[...] = (preact * gate).astype(bf16)
        grad = cotangents[h][...].astype(f32) * gate * (1.0 + preact * (1.0 - gate))
        grad = grad.astype(bf16)
        here = pl.ds(h * rows, rows)
        mean_ref[here, :] = mean
        grad_ref[here, :] = grad
        up_ref[here, :] = (mm_nt(grad, w_neigh[...]) * inverse).astype(bf16)


def node(sums, features, cotangents, degrees, w_self, w_neigh, bias):
    n_part = len(sums)
    rows, width = features[0].shape
    all_rows = jax.ShapeDtypeStruct((rows * n_part, width), bf16)
    shapes = [jax.ShapeDtypeStruct((rows, width), bf16), all_rows, all_rows, all_rows]
    return pl.pallas_call(
        functools.partial(node_kernel, n_part),
        out_shape=shapes,
        in_specs=[VMEM] * (4 * n_part + 3),
        out_specs=[VMEM] * 4,
        compiler_params=params(*sums, *features, *cotangents, w_self, w_neigh, *shapes),
        name="node",
    )(*sums, *features, *cotangents, *degrees, w_self, w_neigh, bias)


def weight_kernel(n_part, place_ref, mean_ref, grad_ref, w_self, *refs):
    features, (keep_ref, send_ref, base_ref) = refs[:n_part], refs[n_part:]
    rows = features[0].shape[0]
    grad_self = mm_tn(features[0][...], grad_ref[pl.ds(0, rows), :])
    for h in range(1, n_part):
        grad_self = grad_self + mm_tn(features[h][...], grad_ref[pl.ds(h * rows, rows), :])
    grad_neigh = mm_tn(mean_ref[...], grad_ref[...])
    first = lax.rem(place_ref[1], 2) == 0
    keep_ref[...] = jnp.where(first, grad_self, grad_neigh)
    send_ref[...] = jnp.where(first, grad_neigh, grad_self).astype(bf16)
    base_ref[...] = mm_nt(grad_ref[pl.ds(0, rows), :], w_self[...])


def weight(place, mean, grad, w_self, features):
    n_part = len(features)
    rows, width = features[0].shape
    return pl.pallas_call(
        functools.partial(weight_kernel, n_part),
        out_shape=[
            jax.ShapeDtypeStruct((width, width), f32),
            jax.ShapeDtypeStruct((width, width), bf16),
            jax.ShapeDtypeStruct((rows, width), f32),
        ],
        in_specs=[SMEM] + [VMEM] * (3 + n_part),
        out_specs=[VMEM] * 3,
        compiler_params=params(mean, grad, w_self, *features),
        name="weight",
    )(place, mean, grad, w_self, *features)


def backward_kernel(n_row, n_part, place_ref, adjacency_ref, mine_ref, other_ref, *refs):
    outs, up_ref = refs[:n_row], refs[n_row]
    rows = outs[0].shape[0]
    row, col = place_ref[0], place_ref[1]
    for h in range(n_part):
        here = pl.ds(h * rows, rows)
        up_ref[span(jnp.bitwise_xor(col, 2 * h), rows), :] = mine_ref[here, :]
        up_ref[span(jnp.bitwise_xor(col, 2 * h + 1), rows), :] = other_ref[here, :]
    for d in list(range(1, n_row)) + [0]:
        block = adjacency_ref[span(jnp.bitwise_xor(row, d), rows), :]
        outs[d][...] = mm(block, up_ref[...]).astype(outs[d].dtype)


def backward(place, adjacency, mine, other, n_row, n_part):
    rows = mine.shape[0] // n_part
    width = mine.shape[1]
    shapes = [jax.ShapeDtypeStruct((rows, width), f32)]
    shapes += [jax.ShapeDtypeStruct((rows, width), bf16)] * (n_row - 1)
    return pl.pallas_call(
        functools.partial(backward_kernel, n_row, n_part),
        out_shape=shapes,
        in_specs=[SMEM] + [VMEM] * 3,
        out_specs=[VMEM] * n_row,
        scratch_shapes=[pltpu.VMEM((2 * n_part * rows, width), bf16)],
        compiler_params=params(adjacency, mine, other, mine, other, *shapes),
        name="backward",
    )(place, adjacency, mine, other)


def exchange(value, axis, distance):
    size = lax.axis_size(axis)
    return lax.ppermute(value, axis, [(i, i ^ distance) for i in range(size)])


def shards(features, grad_out, degrees, w_self, w_neigh, bias, tile_slots, tile_count, tile_masks):
    rows, width = features.shape
    n_row, n_col = lax.axis_size("row"), lax.axis_size("col")
    n_part = n_col // 2
    row, col = lax.axis_index("row"), lax.axis_index("col")
    place = jnp.stack([row, col]).astype(jnp.int32)

    blocks = [features] + [exchange(features, "row", d) for d in range(1, n_row)]
    forms = unpack(
        tile_slots[0, 0], tile_count[0], tile_masks[0, 0], rows * n_row, rows * n_col
    )

    degree_rows = degrees.reshape(rows, 1)
    near_features = [features] + [exchange(features, "col", 2 * h) for h in range(1, n_part)]
    near_cotangents = [grad_out] + [exchange(grad_out, "col", 2 * h) for h in range(1, n_part)]
    near_degrees = [degree_rows] + [
        exchange(degrees, "col", 2 * h).reshape(rows, 1) for h in range(1, n_part)
    ]

    mine, other = forward(place, forms[-1], len(forms) > 1, blocks, n_col)
    other = exchange(other, "col", 1)
    pair = (mine + other.astype(f32)).astype(bf16)
    sums = [pair] + [exchange(pair, "col", 2 * h) for h in range(1, n_part)]

    layer_out, mean, grad, up = node(
        sums, near_features, near_cotangents, near_degrees, w_self, w_neigh, bias.reshape(1, width)
    )
    keep, send, base = weight(place, mean, grad, w_self, near_features)
    up_other = exchange(up, "col", 1)

    backs = backward(place, forms[0], up, up_other, n_row, n_part)
    total = base + backs[0]
    for d in range(1, n_row):
        total = total + exchange(backs[d], "row", d).astype(f32)
    grad_in = total.astype(bf16)

    grads = keep + exchange(send, "col", 1).astype(f32)
    distance = 1
    while distance < n_row:
        rounded = grads.astype(bf16)
        grads = rounded.astype(f32) + exchange(rounded, "row", distance).astype(f32)
        distance *= 2
    grads = grads * (1.0 / math.sqrt(rows * n_row * n_col))
    other_grads = exchange(grads, "col", 1)
    first = lax.rem(col, 2) == 0
    grad_self = jnp.where(first, grads, other_grads)
    grad_neigh = jnp.where(first, other_grads, grads)
    return layer_out, grad_in, grad_self, grad_neigh


def solution(mesh):
    placed = (
        P(("row", "col"), None),
        P(("row", "col"), None),
        P(("row", "col")),
        P(),
        P(),
        P(),
        P("row", "col", None),
        P("row", "col"),
        P("row", "col", None, None, None),
    )
    return jax.shard_map(
        shards,
        mesh=mesh,
        in_specs=placed,
        out_specs=(P(("row", "col"), None), P(("row", "col"), None), P(), P()),
        check_vma=False,
    )
```

```python
import functools
import math

import jax
import jax.numpy as jnp
from jax import lax
from jax.experimental import pallas as pl
from jax.experimental.pallas import tpu as pltpu
from jax.sharding import PartitionSpec as P


BOTH_FORMS_BYTES = 8 * 1024 * 1024
DIGIT_ROWS = 16

VMEM = pl.BlockSpec(memory_space=pltpu.VMEM)
ANY = pl.BlockSpec(memory_space=pl.ANY)
SMEM = pl.BlockSpec(memory_space=pltpu.SMEM)

f32 = jnp.float32
bf16 = jnp.bfloat16


def mm(a, b):
    return jnp.dot(a, b, preferred_element_type=f32)


def mm_nt(a, b):
    return lax.dot_general(a, b, (((1,), (1,)), ((), ())), preferred_element_type=f32)


def mm_tn(a, b):
    return lax.dot_general(a, b, (((0,), (0,)), ((), ())), preferred_element_type=f32)


def params(*arrays):
    held = sum(math.prod(array.shape) * jnp.dtype(array.dtype).itemsize for array in arrays)
    return pltpu.CompilerParams(vmem_limit_bytes=held + held // 8 + (4 << 20))


def cost(nanoseconds):
    return pl.CostEstimate(flops=nanoseconds * 10**6, bytes_accessed=0, transcendentals=0)


def span(index, size):
    return pl.ds(pl.multiple_of(index * size, size), size)


def unpack_kernel(block_rows, gather, slots_ref, count_ref, masks_ref, *refs):
    dense_ref = refs[-1]
    words, width = masks_ref.shape[1:]
    height, length = dense_ref.shape

    @pl.loop(0, height // width)
    def _(step):
        dense_ref[span(step, width), :] = jnp.zeros((width, length), bf16)

    shifts = lax.broadcasted_iota(jnp.int32, (words, 8, width), 1)

    @pl.loop(0, count_ref[0])
    def _(tile):
        slot = slots_ref[tile]
        row_block = lax.rem(slot, block_rows)
        column_block = lax.div(slot, block_rows)
        word = masks_ref[tile]
        spread_words = jnp.broadcast_to(word[:, None, :], (words, 8, width))
        bits = jnp.bitwise_and(jnp.right_shift(spread_words, shifts), 1)
        bits = bits.astype(f32).reshape(words * 8, width)
        if gather:
            dense_ref[span(row_block, width), span(column_block, width)] = bits.T.astype(bf16)
        else:
            dense_ref[span(column_block, width), span(row_block, width)] = bits.astype(bf16)


def unpack(gather, tiles, after, panel, group):
    slot_ids, live_count, masks = tiles
    shape = jax.ShapeDtypeStruct((group, panel) if gather else (panel, group), bf16)
    block_rows = group // masks.shape[2]
    return pl.pallas_call(
        functools.partial(unpack_kernel, block_rows, gather),
        out_shape=shape,
        in_specs=[SMEM, SMEM, VMEM] + [ANY] * len(after),
        out_specs=VMEM,
        compiler_params=params(masks, shape),
        cost_estimate=cost(4000),
        name="unpack_gather" if gather else "unpack_spread",
    )(slot_ids, live_count, masks, *after)


def near_kernel(degrees_ref, features_ref, cotangents_ref, near_ref):
    rows = features_ref.shape[0]
    near_ref[pl.ds(0, rows), :] = features_ref[...]
    near_ref[pl.ds(rows, rows), :] = cotangents_ref[...]
    degree = jnp.broadcast_to(degrees_ref[...], (DIGIT_ROWS, rows))
    place = lax.broadcasted_iota(jnp.int32, degree.shape, 0)
    digit = jnp.bitwise_and(jnp.right_shift(degree, 8 * jnp.minimum(place, 3)), 255)
    near_ref[pl.ds(2 * rows, DIGIT_ROWS), :] = digit.astype(f32).astype(bf16)


def pack_near(degrees, features, cotangents):
    rows, width = features.shape
    near = jax.ShapeDtypeStruct((2 * rows + DIGIT_ROWS, width), bf16)
    return pl.pallas_call(
        near_kernel,
        out_shape=near,
        in_specs=[VMEM] * 3,
        out_specs=VMEM,
        compiler_params=params(near, near),
        cost_estimate=cost(500),
        name="near",
    )(degrees.reshape(1, rows), features, cotangents)


def forward_kernel(n_row, n_col, natural, n_after, place_ref, adjacency_ref, *refs):
    blocks, refs = refs[:n_row], refs[n_row + n_after :]
    outs, panel_ref = refs[:2], refs[2]
    rows = blocks[0].shape[0]
    row, col = place_ref[0], place_ref[1]
    for d in range(n_row):
        panel_ref[span(jnp.bitwise_xor(row, d), rows), :] = blocks[d][...]
    for e in list(range(1, n_col, 2)) + list(range(0, n_col, 2)):
        where = span(jnp.bitwise_xor(col, e), rows)
        if natural:
            total = mm(adjacency_ref[where, :], panel_ref[...])
        else:
            total = mm_tn(adjacency_ref[:, where], panel_ref[...])
        out = outs[e % 2]
        out[pl.ds((e // 2) * rows, rows), :] = total.astype(out.dtype)


def forward(place, adjacency, natural, blocks, after, n_col):
    rows, width = blocks[0].shape
    n_row = len(blocks)
    half = rows * n_col // 2
    shapes = [jax.ShapeDtypeStruct((half, width), kind) for kind in (f32, bf16)]
    return pl.pallas_call(
        functools.partial(forward_kernel, n_row, n_col, natural, len(after)),
        out_shape=shapes,
        in_specs=[SMEM, VMEM] + [VMEM] * n_row + [ANY] * len(after),
        out_specs=[VMEM, VMEM],
        scratch_shapes=[pltpu.VMEM((rows * n_row, width), bf16)],
        compiler_params=params(adjacency, *blocks, *blocks, *shapes),
        cost_estimate=cost(2200),
        name="forward",
    )(place, adjacency, *blocks, *after)


def node_kernel(n_part, *refs):
    sums, refs = refs[:n_part], refs[n_part:]
    nears, refs = refs[:n_part], refs[n_part:]
    w_self, w_neigh, bias, out_ref, mean_ref, grad_ref, up_ref = refs
    rows = out_ref.shape[0]
    for h in range(n_part):
        parts = [sums[h2][pl.ds((h ^ h2) * rows, rows), :].astype(f32) for h2 in range(n_part)]
        while len(parts) > 1:
            parts = [parts[i] + parts[i + 1] for i in range(0, len(parts), 2)]
        digits = nears[h][pl.ds(2 * rows, DIGIT_ROWS), :].astype(f32)[:8, :]
        place = lax.broadcasted_iota(jnp.int32, digits.shape, 0)
        scales = jnp.where(place < 4, jnp.left_shift(1, 8 * jnp.minimum(place, 3)), 0).astype(f32)
        degree = jnp.sum((digits * scales).T, axis=1, keepdims=True)
        inverse = 1.0 / degree
        mean = (parts[0] * inverse).astype(bf16)
        preact = mm(nears[h][pl.ds(0, rows), :], w_self[...]) + mm(mean, w_neigh[...]) + bias[...]
        gate = jax.nn.sigmoid(preact)
        if h == 0:
            out_ref[...] = (preact * gate).astype(bf16)
        grad = nears[h][pl.ds(rows, rows), :].astype(f32) * gate * (1.0 + preact * (1.0 - gate))
        grad = grad.astype(bf16)
        here = pl.ds(h * rows, rows)
        mean_ref[here, :] = mean
        grad_ref[here, :] = grad
        up_ref[here, :] = (mm_nt(grad, w_neigh[...]) * inverse).astype(bf16)


def node(sums, nears, w_self, w_neigh, bias):
    n_part = len(sums)
    width = nears[0].shape[1]
    rows = sums[0].shape[0] // n_part
    all_rows = jax.ShapeDtypeStruct((rows * n_part, width), bf16)
    shapes = [jax.ShapeDtypeStruct((rows, width), bf16), all_rows, all_rows, all_rows]
    return pl.pallas_call(
        functools.partial(node_kernel, n_part),
        out_shape=shapes,
        in_specs=[VMEM] * (2 * n_part + 3),
        out_specs=[VMEM] * 4,
        compiler_params=params(*sums, *nears, w_self, w_neigh, *shapes),
        cost_estimate=cost(2000),
        name="node",
    )(*sums, *nears, w_self, w_neigh, bias)


def weight_kernel(n_part, place_ref, mean_ref, grad_ref, w_self, *refs):
    nears, (keep_ref, send_ref, base_ref, total_ref) = refs[:n_part], refs[n_part:]
    rows = base_ref.shape[0]
    here = pl.ds(0, rows)
    grad_self = mm_tn(nears[0][here, :], grad_ref[here, :])
    for h in range(1, n_part):
        grad_self = grad_self + mm_tn(nears[h][here, :], grad_ref[pl.ds(h * rows, rows), :])
    grad_neigh = mm_tn(mean_ref[...], grad_ref[...])
    first = lax.rem(place_ref[1], 2) == 0
    keep, send = total_ref.at[0], total_ref.at[1]
    keep[...] = jnp.where(first, grad_self, grad_neigh)
    send[...] = jnp.where(first, grad_neigh, grad_self)
    here = span(lax.div(place_ref[1], 2), keep_ref.shape[0])
    keep_ref[...] = keep[here, :]
    send_ref[...] = send[here, :].astype(bf16)
    base_ref[...] = mm_nt(grad_ref[pl.ds(0, rows), :], w_self[...])


def weight(place, mean, grad, w_self, nears):
    n_part = len(nears)
    rows, width = mean.shape[0] // n_part, mean.shape[1]
    return pl.pallas_call(
        functools.partial(weight_kernel, n_part),
        out_shape=[
            jax.ShapeDtypeStruct((width // n_part, width), f32),
            jax.ShapeDtypeStruct((width // n_part, width), bf16),
            jax.ShapeDtypeStruct((rows, width), f32),
        ],
        in_specs=[SMEM] + [VMEM] * (3 + n_part),
        out_specs=[VMEM] * 3,
        scratch_shapes=[pltpu.VMEM((2, width, width), f32)],
        compiler_params=params(mean, grad, w_self, *nears),
        cost_estimate=cost(1300),
        name="weight",
    )(place, mean, grad, w_self, *nears)


def backward_kernel(n_row, n_part, n_after, place_ref, adjacency_ref, mine_ref, other_ref, *refs):
    refs = refs[n_after:]
    outs, up_ref = refs[:n_row], refs[n_row]
    rows = outs[0].shape[0]
    row, col = place_ref[0], place_ref[1]
    for h in range(n_part):
        here = pl.ds(h * rows, rows)
        up_ref[span(jnp.bitwise_xor(col, 2 * h), rows), :] = mine_ref[here, :]
        up_ref[span(jnp.bitwise_xor(col, 2 * h + 1), rows), :] = other_ref[here, :]
    for d in list(range(1, n_row)) + [0]:
        block = adjacency_ref[span(jnp.bitwise_xor(row, d), rows), :]
        outs[d][...] = mm(block, up_ref[...]).astype(outs[d].dtype)


def backward(place, adjacency, mine, other, after, n_row, n_part):
    rows = mine.shape[0] // n_part
    width = mine.shape[1]
    shapes = [jax.ShapeDtypeStruct((rows, width), f32)]
    shapes += [jax.ShapeDtypeStruct((rows, width), bf16)] * (n_row - 1)
    return pl.pallas_call(
        functools.partial(backward_kernel, n_row, n_part, len(after)),
        out_shape=shapes,
        in_specs=[SMEM] + [VMEM] * 3 + [ANY] * len(after),
        out_specs=[VMEM] * n_row,
        scratch_shapes=[pltpu.VMEM((2 * n_part * rows, width), bf16)],
        compiler_params=params(adjacency, mine, other, mine, other, *shapes),
        cost_estimate=cost(1800),
        name="backward",
    )(place, adjacency, mine, other, *after)


def exchange(value, axis, distance):
    size = lax.axis_size(axis)
    return lax.ppermute(value, axis, [(i, i ^ distance) for i in range(size)])


def layer(features, grad_out, degrees, w_self, w_neigh, bias, tile_slots, tile_count, tile_masks):
    rows, width = features.shape
    n_row, n_col = lax.axis_size("row"), lax.axis_size("col")
    n_part = n_col // 2
    row, col = lax.axis_index("row"), lax.axis_index("col")
    place = jnp.stack([row, col]).astype(jnp.int32)
    tiles = (tile_slots[0, 0], tile_count[0], tile_masks[0, 0])
    panel, group = rows * n_row, rows * n_col
    both = 2 * panel * group * 2 <= BOTH_FORMS_BYTES

    blocks = [features] + [None] * (n_row - 1)
    far = sorted(range(2, n_row, 2), key=lambda d: (-(d & -d), d))
    for d in far:
        blocks[d] = exchange(features, "row", d)
    blocks[1] = exchange(features, "row", 1)
    for d in far:
        blocks[d ^ 1] = exchange(blocks[d], "row", 1)
    near = pack_near(degrees, features, grad_out)
    nears = [near] + [exchange(near, "col", 2 * h) for h in range(1, n_part)]

    dense = unpack(both, tiles, [place], panel, group)
    mine, other = forward(place, dense, both, blocks, nears[1:], n_col)
    other = exchange(other, "col", 1)
    pair = (mine + other.astype(f32)).astype(bf16)
    sums = [pair] + [exchange(pair, "col", 2 * h) for h in range(1, n_part)]
    if both:
        dense = unpack(False, tiles, [pair], panel, group)

    layer_out, mean, grad, up = node(sums, nears, w_self, w_neigh, bias.reshape(1, width))
    up_other = exchange(up, "col", 1)
    keep, send, base = weight(place, mean, grad, w_self, nears)
    rounded = (keep + exchange(send, "col", 1).astype(f32)).astype(bf16)
    backs = backward(place, dense, up, up_other, [rounded], n_row, n_part)

    total = base + backs[0].astype(f32)
    pairs = {}
    for d in far + [0]:
        came = exchange(backs[d ^ 1], "row", 1).astype(f32)
        pairs[d] = backs[d].astype(f32) + came if d else total + came
    total = pairs[0]
    for d in far:
        total = total + exchange(pairs[d].astype(bf16), "row", d).astype(f32)
    grad_in = total.astype(bf16)

    distances = [1]
    distance = n_row // 2
    while distance > 1:
        distances.append(distance)
        distance //= 2
    for distance in distances:
        came = exchange(rounded, "row", distance)
        grads = rounded.astype(f32) + came.astype(f32)
        rounded = grads.astype(bf16)
    grads = grads * (1.0 / math.sqrt(panel * n_col))
    slices = [grads] + [exchange(grads, "col", 2 * h) for h in range(1, n_part)]
    part = lax.div(col, 2)
    ordered = []
    for p in range(n_part):
        chosen = slices[0]
        for h in range(1, n_part):
            chosen = jnp.where(jnp.bitwise_xor(part, h) == p, slices[h], chosen)
        ordered.append(chosen)
    grads = jnp.concatenate(ordered, axis=0)
    other_grads = exchange(grads, "col", 1)
    first = lax.rem(col, 2) == 0
    grad_self = jnp.where(first, grads, other_grads)
    grad_neigh = jnp.where(first, other_grads, grads)
    return layer_out, grad_in, grad_self, grad_neigh


def solution(mesh):
    placed = (
        P(("row", "col"), None),
        P(("row", "col"), None),
        P(("row", "col")),
        P(),
        P(),
        P(),
        P("row", "col", None),
        P("row", "col"),
        P("row", "col", None, None, None),
    )
    return jax.shard_map(
        layer,
        mesh=mesh,
        in_specs=placed,
        out_specs=(P(("row", "col"), None), P(("row", "col"), None), P(), P()),
        check_vma=False,
    )
```

```python
import functools
import math

import jax
import jax.numpy as jnp
from jax import lax
from jax.experimental import pallas as pl
from jax.experimental.pallas import tpu as pltpu
from jax.sharding import PartitionSpec as P


BOTH_FORMS_BYTES = 8 * 1024 * 1024
DIGIT_ROWS = 16

VMEM = pl.BlockSpec(memory_space=pltpu.VMEM)
HBM = pl.BlockSpec(memory_space=pltpu.HBM)
ANY = pl.BlockSpec(memory_space=pl.ANY)
SMEM = pl.BlockSpec(memory_space=pltpu.SMEM)

f32 = jnp.float32
bf16 = jnp.bfloat16


def mm(a, b):
    return jnp.dot(a, b, preferred_element_type=f32)


def mm_nt(a, b):
    return lax.dot_general(a, b, (((1,), (1,)), ((), ())), preferred_element_type=f32)


def mm_tn(a, b):
    return lax.dot_general(a, b, (((0,), (0,)), ((), ())), preferred_element_type=f32)


def params(*arrays):
    held = sum(math.prod(array.shape) * jnp.dtype(array.dtype).itemsize for array in arrays)
    return pltpu.CompilerParams(vmem_limit_bytes=held + held // 8 + (4 << 20))


def in_hbm(array):
    return pltpu.with_memory_space_constraint(array, pltpu.HBM)


def cost(nanoseconds):
    return pl.CostEstimate(flops=nanoseconds * 10**6, bytes_accessed=0, transcendentals=0)


def span(index, size):
    return pl.ds(pl.multiple_of(index * size, size), size)


def unpack_kernel(block_rows, gather, split, place_ref, count_ref, slots_hbm, masks_hbm, *refs):
    if split:
        last_ref, refs = refs[-5], refs[:-5] + refs[-4:]
    dense_ref, slots_ref, masks_ref, slots_sem, masks_sem = refs[-5:]
    slots_copy = pltpu.make_async_copy(slots_hbm, slots_ref, slots_sem)
    masks_copy = pltpu.make_async_copy(masks_hbm, masks_ref, masks_sem)
    slots_copy.start()
    masks_copy.start()
    tiles, words, width = masks_ref.shape
    height, length = dense_ref.shape
    together = math.gcd(tiles, 8)

    @pl.loop(0, height // width)
    def _(step):
        dense_ref[span(step, width), :] = jnp.zeros((width, length), bf16)

    if split:

        @pl.loop(0, last_ref.shape[0] // width)
        def _(step):
            last_ref[span(step, width), :] = jnp.zeros((width, length), bf16)

    slots_copy.wait()
    masks_copy.wait()

    def blocks(tile):
        slot = slots_ref[0, tile]
        return lax.rem(slot, block_rows), lax.div(slot, block_rows)

    if not gather:
        shifts = lax.broadcasted_iota(jnp.int32, (words, 8, width), 1)

        @pl.loop(0, count_ref[0])
        def _(tile):
            row_block, column_block = blocks(tile)
            word = jnp.broadcast_to(masks_ref[tile][:, None, :], (words, 8, width))
            bits = jnp.bitwise_and(jnp.right_shift(word, shifts), 1)
            bits = bits.astype(f32).reshape(words * 8, width).astype(bf16)
            if not split:
                dense_ref[span(column_block, width), span(row_block, width)] = bits
                return
            own, within = lax.div(column_block, split), lax.rem(column_block, split)
            spot = jnp.bitwise_xor(place_ref[0], own) * split + within
            edge = height // width

            @pl.when(spot < edge)
            def _():
                dense_ref[span(spot, width), span(row_block, width)] = bits

            @pl.when(spot >= edge)
            def _():
                last_ref[span(spot - edge, width), span(row_block, width)] = bits

        return

    stacked = together * words
    source = lax.broadcasted_iota(jnp.int32, (stacked, together * words * 8), 0)
    target = lax.broadcasted_iota(jnp.int32, (stacked, together * words * 8), 1)
    repeat = (source == lax.div(target, 8)).astype(f32).astype(bf16)
    shifts = lax.rem(lax.broadcasted_iota(jnp.int32, (width, words * 8), 1), 8)

    @pl.loop(0, lax.div(count_ref[0] + together - 1, together))
    def _(step):
        first = step * together
        live = [
            masks_ref[first + t] * (first + t < count_ref[0]).astype(jnp.int32)
            for t in range(together)
        ]
        turned = jnp.concatenate(live, axis=0).astype(f32).T.astype(bf16)
        word = mm(turned, repeat)
        for t in range(together):
            row_block, column_block = blocks(first + t)
            own = word[:, t * words * 8 : (t + 1) * words * 8].astype(jnp.int32)
            bits = jnp.bitwise_and(jnp.right_shift(own, shifts), 1).astype(f32).astype(bf16)
            dense_ref[span(row_block, width), span(column_block, width)] = bits


def unpack(gather, place, tiles, after, panel, group, rows=0):
    slot_ids, live_count, masks = tiles
    width = masks.shape[2]
    heights = [panel - 2 * rows, 2 * rows] if rows else [group if gather else panel]
    shapes = [jax.ShapeDtypeStruct((h, panel if gather else group), bf16) for h in heights]
    return pl.pallas_call(
        functools.partial(unpack_kernel, group // width, gather, rows // width),
        out_shape=shapes,
        in_specs=[SMEM, SMEM, HBM, HBM] + [ANY] * len(after),
        out_specs=[VMEM] * len(shapes),
        scratch_shapes=[
            pltpu.SMEM(slot_ids.shape, jnp.int32),
            pltpu.VMEM(masks.shape, jnp.int32),
            pltpu.SemaphoreType.DMA,
            pltpu.SemaphoreType.DMA,
        ],
        compiler_params=params(masks, *shapes),
        cost_estimate=cost(2000),
        name="unpack_gather" if gather else "unpack_spread",
    )(place, live_count, in_hbm(slot_ids), in_hbm(masks), *after)


def near_kernel(degrees_hbm, features_hbm, cotangents_hbm, near_ref, degrees_ref, sems):
    rows = features_hbm.shape[0]
    copies = [
        pltpu.make_async_copy(degrees_hbm, degrees_ref, sems.at[0]),
        pltpu.make_async_copy(features_hbm, near_ref.at[pl.ds(0, rows), :], sems.at[1]),
        pltpu.make_async_copy(cotangents_hbm, near_ref.at[pl.ds(rows, rows), :], sems.at[2]),
    ]
    for copy in copies:
        copy.start()
    copies[0].wait()
    degree = jnp.broadcast_to(degrees_ref[...], (DIGIT_ROWS, rows))
    place = lax.broadcasted_iota(jnp.int32, degree.shape, 0)
    digit = jnp.bitwise_and(jnp.right_shift(degree, 8 * jnp.minimum(place, 3)), 255)
    near_ref[pl.ds(2 * rows, DIGIT_ROWS), :] = digit.astype(f32).astype(bf16)
    copies[1].wait()
    copies[2].wait()


def pack_near(degrees, features, cotangents):
    rows, width = features.shape
    near = jax.ShapeDtypeStruct((2 * rows + DIGIT_ROWS, width), bf16)
    return pl.pallas_call(
        near_kernel,
        out_shape=near,
        in_specs=[HBM] * 3,
        out_specs=VMEM,
        scratch_shapes=[pltpu.VMEM((1, rows), jnp.int32), pltpu.SemaphoreType.DMA((3,))],
        compiler_params=params(near, near),
        cost_estimate=cost(500),
        name="near",
    )(in_hbm(degrees.reshape(1, rows)), in_hbm(features), in_hbm(cotangents))


def forward_kernel(distances, n_col, natural, last, place_ref, adjacency_ref, *refs):
    blocks, refs = refs[: len(distances)], refs[len(distances) :]
    rows = blocks[0].shape[0]
    row, col = place_ref[0], place_ref[1]
    for e in list(range(1, n_col, 2)) + list(range(0, n_col, 2)):
        own = span(jnp.bitwise_xor(col, e), rows)
        total = refs[0][pl.ds(e * rows, rows), :] if last else None
        for d, block in zip(distances, blocks):
            panel = span(jnp.bitwise_xor(row, d), rows)
            if natural:
                term = mm(adjacency_ref[own, panel], block[...])
            else:
                term = mm_tn(adjacency_ref[panel, own], block[...])
            total = term if total is None else total + term
        if last:
            out = refs[1 + e % 2]
            out[pl.ds((e // 2) * rows, rows), :] = total.astype(out.dtype)
        else:
            refs[0][pl.ds(e * rows, rows), :] = total


def forward(place, adjacency, natural, blocks, total, n_col):
    distances, arrays = list(blocks), list(blocks.values())
    rows, width = arrays[0].shape
    last = total is not None
    if last:
        half = rows * n_col // 2
        shapes = [jax.ShapeDtypeStruct((half, width), kind) for kind in (f32, bf16)]
    else:
        shapes = [jax.ShapeDtypeStruct((rows * n_col, width), f32)]
    inputs = arrays + ([total] if last else [])
    return pl.pallas_call(
        functools.partial(forward_kernel, distances, n_col, natural, last),
        out_shape=shapes,
        in_specs=[SMEM] + [VMEM] * (1 + len(inputs)),
        out_specs=[VMEM] * len(shapes),
        compiler_params=params(adjacency, *inputs, *shapes),
        cost_estimate=cost(250 * len(distances)),
        name="forward_last" if last else "forward",
    )(place, adjacency, *inputs)


def node_kernel(n_part, *refs):
    sums, refs = refs[:n_part], refs[n_part:]
    nears, refs = refs[:n_part], refs[n_part:]
    w_self, w_neigh, bias, out_ref, mean_ref, grad_ref, up_ref = refs
    rows = out_ref.shape[0]
    for h in range(n_part):
        parts = [sums[h2][pl.ds((h ^ h2) * rows, rows), :].astype(f32) for h2 in range(n_part)]
        while len(parts) > 1:
            parts = [parts[i] + parts[i + 1] for i in range(0, len(parts), 2)]
        digits = nears[h][pl.ds(2 * rows, DIGIT_ROWS), :].astype(f32)[:8, :]
        place = lax.broadcasted_iota(jnp.int32, digits.shape, 0)
        scales = jnp.where(place < 4, jnp.left_shift(1, 8 * jnp.minimum(place, 3)), 0).astype(f32)
        degree = jnp.sum((digits * scales).T, axis=1, keepdims=True)
        inverse = 1.0 / degree
        mean = (parts[0] * inverse).astype(bf16)
        preact = mm(nears[h][pl.ds(0, rows), :], w_self[...]) + mm(mean, w_neigh[...]) + bias[...]
        gate = jax.nn.sigmoid(preact)
        if h == 0:
            out_ref[...] = (preact * gate).astype(bf16)
        grad = nears[h][pl.ds(rows, rows), :].astype(f32) * gate * (1.0 + preact * (1.0 - gate))
        grad = grad.astype(bf16)
        here = pl.ds(h * rows, rows)
        mean_ref[here, :] = mean
        grad_ref[here, :] = grad
        up_ref[here, :] = (mm_nt(grad, w_neigh[...]) * inverse).astype(bf16)


def node(sums, nears, w_self, w_neigh, bias):
    n_part = len(sums)
    width = nears[0].shape[1]
    rows = sums[0].shape[0] // n_part
    all_rows = jax.ShapeDtypeStruct((rows * n_part, width), bf16)
    shapes = [jax.ShapeDtypeStruct((rows, width), bf16), all_rows, all_rows, all_rows]
    return pl.pallas_call(
        functools.partial(node_kernel, n_part),
        out_shape=shapes,
        in_specs=[VMEM] * (2 * n_part + 3),
        out_specs=[VMEM] * 4,
        compiler_params=params(*sums, *nears, w_self, w_neigh, *shapes),
        cost_estimate=cost(2000),
        name="node",
    )(*sums, *nears, w_self, w_neigh, bias)


def weight_kernel(n_part, place_ref, mean_ref, grad_ref, w_self, *refs):
    nears, (slice_ref, base_ref, total_ref) = refs[:n_part], refs[n_part:]
    rows = base_ref.shape[0]
    here = pl.ds(0, rows)
    grad_self = mm_tn(nears[0][here, :], grad_ref[here, :])
    for h in range(1, n_part):
        grad_self = grad_self + mm_tn(nears[h][here, :], grad_ref[pl.ds(h * rows, rows), :])
    grad_neigh = mm_tn(mean_ref[...], grad_ref[...])
    total_ref[0], total_ref[1] = grad_self, grad_neigh
    here = span(lax.div(place_ref[1], 2), slice_ref.shape[1])
    slice_ref[0] = total_ref[0, here, :].astype(bf16)
    slice_ref[1] = total_ref[1, here, :].astype(bf16)
    base_ref[...] = mm_nt(grad_ref[pl.ds(0, rows), :], w_self[...])


def weight(place, mean, grad, w_self, nears):
    n_part = len(nears)
    rows, width = mean.shape[0] // n_part, mean.shape[1]
    return pl.pallas_call(
        functools.partial(weight_kernel, n_part),
        out_shape=[
            jax.ShapeDtypeStruct((2, width // n_part, width), bf16),
            jax.ShapeDtypeStruct((rows, width), f32),
        ],
        in_specs=[SMEM] + [VMEM] * (3 + n_part),
        out_specs=[VMEM] * 2,
        scratch_shapes=[pltpu.VMEM((2, width, width), f32)],
        compiler_params=params(mean, grad, w_self, *nears),
        cost_estimate=cost(1300),
        name="weight",
    )(place, mean, grad, w_self, *nears)


def backward_kernel(distances, n_part, n_after, place_ref, adjacency_ref, mine_ref, other_ref, *refs):
    outs, up_ref = refs[n_after:-1], refs[-1]
    rows = outs[0].shape[0]
    row, col = place_ref[0], place_ref[1]
    for h in range(n_part):
        here = pl.ds(h * rows, rows)
        up_ref[span(jnp.bitwise_xor(col, 2 * h), rows), :] = mine_ref[here, :]
        up_ref[span(jnp.bitwise_xor(col, 2 * h + 1), rows), :] = other_ref[here, :]
    whole = adjacency_ref.shape[0] > len(distances) * rows
    for index, (d, out) in enumerate(zip(distances, outs)):
        if whole:
            block = adjacency_ref[span(jnp.bitwise_xor(row, d), rows), :]
        else:
            block = adjacency_ref[pl.ds(index * rows, rows), :]
        out[...] = mm(block, up_ref[...]).astype(out.dtype)


def backward(place, adjacency, mine, other, after, distances, n_part):
    rows = mine.shape[0] // n_part
    width = mine.shape[1]
    shapes = [jax.ShapeDtypeStruct((rows, width), bf16 if d else f32) for d in distances]
    outs = pl.pallas_call(
        functools.partial(backward_kernel, distances, n_part, len(after)),
        out_shape=shapes,
        in_specs=[SMEM] + [VMEM] * 3 + [ANY] * len(after),
        out_specs=[VMEM] * len(shapes),
        scratch_shapes=[pltpu.VMEM((2 * n_part * rows, width), bf16)],
        compiler_params=params(adjacency, mine, other, mine, other, *shapes),
        cost_estimate=cost(200 * len(distances)),
        name="backward" if 0 in distances else "backward_far",
    )(place, adjacency, mine, other, *after)
    return dict(zip(distances, outs))


def final_kernel(n_part, n_terms, scale, place_ref, *refs):
    terms, refs = refs[:n_terms], refs[n_terms:]
    mine, others, refs = refs[:n_part], refs[n_part : 2 * n_part], refs[2 * n_part :]
    grad_in_ref, self_ref, neigh_ref = refs
    total = terms[0][...]
    for term in terms[1:]:
        total = total + term[...].astype(f32)
    grad_in_ref[...] = total.astype(bf16)
    first = lax.rem(place_ref[1], 2) == 0
    for h in range(n_part):
        here = span(jnp.bitwise_xor(lax.div(place_ref[1], 2), h), mine[h].shape[0])
        one, two = mine[h][...] * scale, others[h][...] * scale
        self_ref[here, :] = jnp.where(first, one, two)
        neigh_ref[here, :] = jnp.where(first, two, one)


def final(place, terms, mine, others, scale):
    n_part = len(mine)
    rows, width = terms[0].shape
    shapes = [
        jax.ShapeDtypeStruct((rows, width), bf16),
        jax.ShapeDtypeStruct((width, width), f32),
        jax.ShapeDtypeStruct((width, width), f32),
    ]
    return pl.pallas_call(
        functools.partial(final_kernel, n_part, len(terms), scale),
        out_shape=shapes,
        in_specs=[SMEM] + [VMEM] * (len(terms) + 2 * n_part),
        out_specs=[VMEM] * 3,
        compiler_params=params(*terms, *mine, *others, *shapes),
        cost_estimate=cost(800),
        name="final",
    )(place, *terms, *mine, *others)


def exchange(value, axis, distance):
    size = lax.axis_size(axis)
    return lax.ppermute(value, axis, [(i, i ^ distance) for i in range(size)])


def layer(features, grad_out, degrees, w_self, w_neigh, bias, tile_slots, tile_count, tile_masks):
    rows, width = features.shape
    n_row, n_col = lax.axis_size("row"), lax.axis_size("col")
    n_part = n_col // 2
    row, col = lax.axis_index("row"), lax.axis_index("col")
    place = jnp.stack([row, col]).astype(jnp.int32)
    tiles = (tile_slots[0], tile_count[0], tile_masks[0, 0])
    panel, group = rows * n_row, rows * n_col
    both = 2 * panel * group * 2 <= BOTH_FORMS_BYTES

    blocks = [features] + [None] * (n_row - 1)
    far = sorted(range(2, n_row, 2), key=lambda d: (-(d & -d), d))
    for d in far:
        blocks[d] = exchange(features, "row", d)
    blocks[1] = exchange(features, "row", 1)
    for d in far:
        blocks[d ^ 1] = exchange(blocks[d], "row", 1)
    near = pack_near(degrees, features, grad_out)
    nears = [near] + [exchange(near, "col", 2 * h) for h in range(1, n_part)]

    (dense,) = unpack(both, place, tiles, [], panel, group)
    late = far[-1] ^ 1
    early = {d: blocks[d] for d in range(n_row) if d != late}
    (total,) = forward(place, dense, both, early, None, n_col)
    mine, other = forward(place, dense, both, {late: blocks[late]}, total, n_col)
    other = exchange(other, "col", 1)
    pair = (mine + other.astype(f32)).astype(bf16)
    sums = [pair] + [exchange(pair, "col", 2 * h) for h in range(1, n_part)]

    layer_out, mean, grad, up = node(sums, nears, w_self, w_neigh, bias.reshape(1, width))
    up_other = exchange(up, "col", 1)
    slices, base = weight(place, mean, grad, w_self, nears)
    every = list(range(n_row))
    if both:
        near_part, far_part = unpack(False, place, tiles, [pair], panel, group, rows)
        backs = backward(place, far_part, up, up_other, [slices], every[-2:], n_part)
        backs.update(backward(place, near_part, up, up_other, [], every[:-2], n_part))
    else:
        backs = backward(place, dense, up, up_other, [slices], every, n_part)

    terms = [base, backs[0]]
    for d in reversed(far):
        came = exchange(backs[d ^ 1], "row", 1)
        both_x = (backs[d].astype(f32) + came.astype(f32)).astype(bf16)
        terms.append(exchange(both_x, "row", d))
    terms.append(exchange(backs[1], "row", 1))

    sums = slices.astype(f32) + exchange(slices, "row", 1).astype(f32)
    core = lax.rem(col, 2) == 0
    keep = jnp.where(core, sums[0], sums[1])
    send = jnp.where(core, sums[1], sums[0]).astype(bf16)
    grads = keep + exchange(send, "col", 1).astype(f32)
    distance = n_row // 2
    while distance > 1:
        rounded = grads.astype(bf16)
        came = exchange(rounded, "row", distance)
        grads = rounded.astype(f32) + came.astype(f32)
        distance //= 2
    mine = [grads] + [exchange(grads, "col", 2 * h) for h in range(1, n_part)]
    others = [exchange(value, "col", 1) for value in mine]
    scale = 1.0 / math.sqrt(panel * n_col)
    grad_in, grad_self, grad_neigh = final(place, terms, mine, others, scale)
    return layer_out, grad_in, grad_self, grad_neigh


def solution(mesh):
    placed = (
        P(("row", "col"), None),
        P(("row", "col"), None),
        P(("row", "col")),
        P(),
        P(),
        P(),
        P("row", "col", None),
        P("row", "col"),
        P("row", "col", None, None, None),
    )
    return jax.shard_map(
        layer,
        mesh=mesh,
        in_specs=placed,
        out_specs=(P(("row", "col"), None), P(("row", "col"), None), P(), P()),
        check_vma=False,
    )
```

```python
import functools
import math

import jax
import jax.numpy as jnp
from jax import lax
from jax.experimental import pallas as pl
from jax.experimental.pallas import tpu as pltpu
from jax.sharding import PartitionSpec as P


BOTH_FORMS_BYTES = 8 * 1024 * 1024
DIGIT_ROWS = 16

VMEM = pl.BlockSpec(memory_space=pltpu.VMEM)
HBM = pl.BlockSpec(memory_space=pltpu.HBM)
ANY = pl.BlockSpec(memory_space=pl.ANY)
SMEM = pl.BlockSpec(memory_space=pltpu.SMEM)

f32 = jnp.float32
bf16 = jnp.bfloat16


def mm(a, b):
    return jnp.dot(a, b, preferred_element_type=f32)


def mm_nt(a, b):
    return lax.dot_general(a, b, (((1,), (1,)), ((), ())), preferred_element_type=f32)


def mm_tn(a, b):
    return lax.dot_general(a, b, (((0,), (0,)), ((), ())), preferred_element_type=f32)


def params(*arrays):
    held = sum(math.prod(array.shape) * jnp.dtype(array.dtype).itemsize for array in arrays)
    return pltpu.CompilerParams(vmem_limit_bytes=held + held // 8 + (4 << 20))


def in_hbm(array):
    return pltpu.with_memory_space_constraint(array, pltpu.HBM)


def cost(nanoseconds):
    return pl.CostEstimate(flops=nanoseconds * 10**6, bytes_accessed=0, transcendentals=0)


def span(index, size):
    return pl.ds(pl.multiple_of(index * size, size), size)


def unpack_kernel(block_rows, gather, split, place_ref, count_ref, slots_hbm, masks_hbm, *refs):
    if split:
        last_ref, refs = refs[-5], refs[:-5] + refs[-4:]
    dense_ref, slots_ref, masks_ref, slots_sem, masks_sem = refs[-5:]
    slots_copy = pltpu.make_async_copy(slots_hbm, slots_ref, slots_sem)
    masks_copy = pltpu.make_async_copy(masks_hbm, masks_ref, masks_sem)
    slots_copy.start()
    masks_copy.start()
    tiles, words, width = masks_ref.shape
    height, length = dense_ref.shape
    together = math.gcd(tiles, 8)

    @pl.loop(0, height // width)
    def _(step):
        dense_ref[span(step, width), :] = jnp.zeros((width, length), bf16)

    if split:

        @pl.loop(0, last_ref.shape[0] // width)
        def _(step):
            last_ref[span(step, width), :] = jnp.zeros((width, length), bf16)

    slots_copy.wait()
    masks_copy.wait()

    def blocks(tile):
        slot = slots_ref[0, tile]
        return lax.rem(slot, block_rows), lax.div(slot, block_rows)

    if not gather:
        shifts = lax.broadcasted_iota(jnp.int32, (words, 8, width), 1)

        @pl.loop(0, count_ref[0])
        def _(tile):
            row_block, column_block = blocks(tile)
            word = jnp.broadcast_to(masks_ref[tile][:, None, :], (words, 8, width))
            bits = jnp.bitwise_and(jnp.right_shift(word, shifts), 1)
            bits = bits.astype(f32).reshape(words * 8, width).astype(bf16)
            if not split:
                dense_ref[span(column_block, width), span(row_block, width)] = bits
                return
            own, within = lax.div(column_block, split), lax.rem(column_block, split)
            spot = jnp.bitwise_xor(place_ref[0], own) * split + within
            edge = height // width

            @pl.when(spot < edge)
            def _():
                dense_ref[span(spot, width), span(row_block, width)] = bits

            @pl.when(spot >= edge)
            def _():
                last_ref[span(spot - edge, width), span(row_block, width)] = bits

        return

    places = jnp.left_shift(1, lax.broadcasted_iota(jnp.int32, (words, 8, width), 1))

    @pl.loop(0, lax.div(count_ref[0] + together - 1, together))
    def _(step):
        for t in range(together):
            tile = step * together + t
            row_block, column_block = blocks(tile)
            word = masks_ref[tile] * (tile < count_ref[0]).astype(jnp.int32)
            word = jnp.broadcast_to(word[:, None, :], (words, 8, width))
            bits = jnp.where(jnp.bitwise_and(word, places) != 0, 1.0, 0.0).astype(f32)
            bits = bits.reshape(words * 8, width).astype(bf16)
            dense_ref[span(row_block, width), span(column_block, width)] = bits.T


def unpack(gather, place, tiles, after, panel, group, rows=0):
    slot_ids, live_count, masks = tiles
    width = masks.shape[2]
    heights = [panel - 2 * rows, 2 * rows] if rows else [group if gather else panel]
    shapes = [jax.ShapeDtypeStruct((h, panel if gather else group), bf16) for h in heights]
    return pl.pallas_call(
        functools.partial(unpack_kernel, group // width, gather, rows // width),
        out_shape=shapes,
        in_specs=[SMEM, SMEM, HBM, HBM] + [ANY] * len(after),
        out_specs=[VMEM] * len(shapes),
        scratch_shapes=[
            pltpu.SMEM(slot_ids.shape, jnp.int32),
            pltpu.VMEM(masks.shape, jnp.int32),
            pltpu.SemaphoreType.DMA,
            pltpu.SemaphoreType.DMA,
        ],
        compiler_params=params(masks, *shapes),
        cost_estimate=cost(2000),
        name="unpack_gather" if gather else "unpack_spread",
    )(place, live_count, in_hbm(slot_ids), in_hbm(masks), *after)


def near_kernel(degrees_hbm, features_hbm, cotangents_hbm, near_ref, degrees_ref, sems):
    rows = features_hbm.shape[0]
    copies = [
        pltpu.make_async_copy(degrees_hbm, degrees_ref, sems.at[0]),
        pltpu.make_async_copy(features_hbm, near_ref.at[pl.ds(0, rows), :], sems.at[1]),
        pltpu.make_async_copy(cotangents_hbm, near_ref.at[pl.ds(rows, rows), :], sems.at[2]),
    ]
    for copy in copies:
        copy.start()
    copies[0].wait()
    degree = jnp.broadcast_to(degrees_ref[...], (DIGIT_ROWS, rows))
    place = lax.broadcasted_iota(jnp.int32, degree.shape, 0)
    digit = jnp.bitwise_and(jnp.right_shift(degree, 8 * jnp.minimum(place, 3)), 255)
    near_ref[pl.ds(2 * rows, DIGIT_ROWS), :] = digit.astype(f32).astype(bf16)
    copies[1].wait()
    copies[2].wait()


def pack_near(degrees, features, cotangents):
    rows, width = features.shape
    near = jax.ShapeDtypeStruct((2 * rows + DIGIT_ROWS, width), bf16)
    return pl.pallas_call(
        near_kernel,
        out_shape=near,
        in_specs=[HBM] * 3,
        out_specs=VMEM,
        scratch_shapes=[pltpu.VMEM((1, rows), jnp.int32), pltpu.SemaphoreType.DMA((3,))],
        compiler_params=params(near, near),
        cost_estimate=cost(500),
        name="near",
    )(in_hbm(degrees.reshape(1, rows)), in_hbm(features), in_hbm(cotangents))


def forward_kernel(distances, n_col, natural, last, place_ref, adjacency_ref, *refs):
    blocks, refs = refs[: len(distances)], refs[len(distances) :]
    rows = blocks[0].shape[0]
    row, col = place_ref[0], place_ref[1]
    for e in list(range(1, n_col, 2)) + list(range(0, n_col, 2)):
        own = span(jnp.bitwise_xor(col, e), rows)
        total = refs[0][pl.ds(e * rows, rows), :] if last else None
        for d, block in zip(distances, blocks):
            panel = span(jnp.bitwise_xor(row, d), rows)
            if natural:
                term = mm(adjacency_ref[own, panel], block[...])
            else:
                term = mm_tn(adjacency_ref[panel, own], block[...])
            total = term if total is None else total + term
        if last:
            out = refs[1 + e % 2]
            out[pl.ds((e // 2) * rows, rows), :] = total.astype(out.dtype)
        else:
            refs[0][pl.ds(e * rows, rows), :] = total


def forward(place, adjacency, natural, blocks, total, n_col):
    distances, arrays = list(blocks), list(blocks.values())
    rows, width = arrays[0].shape
    last = total is not None
    if last:
        half = rows * n_col // 2
        shapes = [jax.ShapeDtypeStruct((half, width), kind) for kind in (f32, bf16)]
    else:
        shapes = [jax.ShapeDtypeStruct((rows * n_col, width), f32)]
    inputs = arrays + ([total] if last else [])
    return pl.pallas_call(
        functools.partial(forward_kernel, distances, n_col, natural, last),
        out_shape=shapes,
        in_specs=[SMEM] + [VMEM] * (1 + len(inputs)),
        out_specs=[VMEM] * len(shapes),
        compiler_params=params(adjacency, *inputs, *shapes),
        cost_estimate=cost(250 * len(distances)),
        name="forward_last" if last else "forward",
    )(place, adjacency, *inputs)


def node_kernel(n_part, *refs):
    sums, refs = refs[:n_part], refs[n_part:]
    nears, refs = refs[:n_part], refs[n_part:]
    w_self, w_neigh, bias, out_ref, mean_ref, grad_ref, up_ref = refs
    rows = out_ref.shape[0]
    for h in range(n_part):
        parts = [sums[h2][pl.ds((h ^ h2) * rows, rows), :].astype(f32) for h2 in range(n_part)]
        while len(parts) > 1:
            parts = [parts[i] + parts[i + 1] for i in range(0, len(parts), 2)]
        digits = nears[h][pl.ds(2 * rows, DIGIT_ROWS), :].astype(f32)[:8, :]
        place = lax.broadcasted_iota(jnp.int32, digits.shape, 0)
        scales = jnp.where(place < 4, jnp.left_shift(1, 8 * jnp.minimum(place, 3)), 0).astype(f32)
        degree = jnp.sum((digits * scales).T, axis=1, keepdims=True)
        inverse = 1.0 / degree
        mean = (parts[0] * inverse).astype(bf16)
        preact = mm(nears[h][pl.ds(0, rows), :], w_self[...]) + mm(mean, w_neigh[...]) + bias[...]
        gate = jax.nn.sigmoid(preact)
        if h == 0:
            out_ref[...] = (preact * gate).astype(bf16)
        grad = nears[h][pl.ds(rows, rows), :].astype(f32) * gate * (1.0 + preact * (1.0 - gate))
        grad = grad.astype(bf16)
        here = pl.ds(h * rows, rows)
        mean_ref[here, :] = mean
        grad_ref[here, :] = grad
        up_ref[here, :] = (mm_nt(grad, w_neigh[...]) * inverse).astype(bf16)


def node(sums, nears, w_self, w_neigh, bias):
    n_part = len(sums)
    width = nears[0].shape[1]
    rows = sums[0].shape[0] // n_part
    all_rows = jax.ShapeDtypeStruct((rows * n_part, width), bf16)
    shapes = [jax.ShapeDtypeStruct((rows, width), bf16), all_rows, all_rows, all_rows]
    return pl.pallas_call(
        functools.partial(node_kernel, n_part),
        out_shape=shapes,
        in_specs=[VMEM] * (2 * n_part + 3),
        out_specs=[VMEM] * 4,
        compiler_params=params(*sums, *nears, w_self, w_neigh, *shapes),
        cost_estimate=cost(2000),
        name="node",
    )(*sums, *nears, w_self, w_neigh, bias)


def weight_kernel(n_part, place_ref, mean_ref, grad_ref, w_self, *refs):
    nears, (slice_ref, base_ref, total_ref) = refs[:n_part], refs[n_part:]
    rows = base_ref.shape[0]
    here = pl.ds(0, rows)
    grad_self = mm_tn(nears[0][here, :], grad_ref[here, :])
    for h in range(1, n_part):
        grad_self = grad_self + mm_tn(nears[h][here, :], grad_ref[pl.ds(h * rows, rows), :])
    grad_neigh = mm_tn(mean_ref[...], grad_ref[...])
    total_ref[0], total_ref[1] = grad_self, grad_neigh
    here = span(lax.div(place_ref[1], 2), slice_ref.shape[1])
    slice_ref[0] = total_ref[0, here, :].astype(bf16)
    slice_ref[1] = total_ref[1, here, :].astype(bf16)
    base_ref[...] = mm_nt(grad_ref[pl.ds(0, rows), :], w_self[...])


def weight(place, mean, grad, w_self, nears):
    n_part = len(nears)
    rows, width = mean.shape[0] // n_part, mean.shape[1]
    return pl.pallas_call(
        functools.partial(weight_kernel, n_part),
        out_shape=[
            jax.ShapeDtypeStruct((2, width // n_part, width), bf16),
            jax.ShapeDtypeStruct((rows, width), f32),
        ],
        in_specs=[SMEM] + [VMEM] * (3 + n_part),
        out_specs=[VMEM] * 2,
        scratch_shapes=[pltpu.VMEM((2, width, width), f32)],
        compiler_params=params(mean, grad, w_self, *nears),
        cost_estimate=cost(1300),
        name="weight",
    )(place, mean, grad, w_self, *nears)


def backward_kernel(groups, place_of, n_part, n_after, place_ref, adjacency_ref, mine_ref, other_ref, *refs):
    outs, up_ref = refs[n_after:-1], refs[-1]
    rows = mine_ref.shape[0] // n_part
    row, col = place_ref[0], place_ref[1]
    for h in range(n_part):
        here = pl.ds(h * rows, rows)
        up_ref[span(jnp.bitwise_xor(col, 2 * h), rows), :] = mine_ref[here, :]
        up_ref[span(jnp.bitwise_xor(col, 2 * h + 1), rows), :] = other_ref[here, :]
    for group, out in zip(groups, outs):
        for index, d in enumerate(group):
            if place_of is None:
                where = span(jnp.bitwise_xor(row, d), rows)
            else:
                where = pl.ds(place_of[d] * rows, rows)
            product = mm(adjacency_ref[where, :], up_ref[...])
            out[pl.ds(index * rows, rows), :] = product.astype(out.dtype)


def backward(place, adjacency, place_of, mine, other, after, groups, n_part):
    rows = mine.shape[0] // n_part
    width = mine.shape[1]
    shapes = [
        jax.ShapeDtypeStruct((len(group) * rows, width), f32 if group == (0,) else bf16)
        for group in groups
    ]
    outs = pl.pallas_call(
        functools.partial(backward_kernel, groups, place_of, n_part, len(after)),
        out_shape=shapes,
        in_specs=[SMEM] + [VMEM] * 3 + [ANY] * len(after),
        out_specs=[VMEM] * len(shapes),
        scratch_shapes=[pltpu.VMEM((2 * n_part * rows, width), bf16)],
        compiler_params=params(adjacency, mine, other, mine, other, *shapes),
        cost_estimate=cost(200 * sum(len(group) for group in groups)),
        name="backward" if (0,) in groups else "backward_far",
    )(place, adjacency, mine, other, *after)
    return dict(zip(groups, outs))


def join_kernel(n_part, scale, place_ref, *refs):
    mine, others, (self_ref, neigh_ref) = refs[:n_part], refs[n_part:-2], refs[-2:]
    first = lax.rem(place_ref[1], 2) == 0
    for h in range(n_part):
        here = span(jnp.bitwise_xor(lax.div(place_ref[1], 2), h), mine[h].shape[0])
        one, two = mine[h][...] * scale, others[h][...] * scale
        self_ref[here, :] = jnp.where(first, one, two)
        neigh_ref[here, :] = jnp.where(first, two, one)


def join(place, mine, others, scale):
    n_part = len(mine)
    width = mine[0].shape[1]
    shapes = [jax.ShapeDtypeStruct((width, width), f32)] * 2
    return pl.pallas_call(
        functools.partial(join_kernel, n_part, scale),
        out_shape=shapes,
        in_specs=[SMEM] + [VMEM] * (2 * n_part),
        out_specs=[VMEM] * 2,
        compiler_params=params(*mine, *others, *shapes),
        cost_estimate=cost(800),
        name="join",
    )(place, *mine, *others)


def exchange(value, axis, distance):
    size = lax.axis_size(axis)
    return lax.ppermute(value, axis, [(i, i ^ distance) for i in range(size)])


def layer(features, grad_out, degrees, w_self, w_neigh, bias, tile_slots, tile_count, tile_masks):
    rows, width = features.shape
    n_row, n_col = lax.axis_size("row"), lax.axis_size("col")
    n_part = n_col // 2
    row, col = lax.axis_index("row"), lax.axis_index("col")
    place = jnp.stack([row, col]).astype(jnp.int32)
    tiles = (tile_slots[0], tile_count[0], tile_masks[0, 0])
    panel, group = rows * n_row, rows * n_col
    both = 2 * panel * group * 2 <= BOTH_FORMS_BYTES

    blocks = [features] + [None] * (n_row - 1)
    far = sorted(range(2, n_row, 2), key=lambda d: (-(d & -d), d))
    for d in far:
        blocks[d] = exchange(features, "row", d)
    blocks[1] = exchange(features, "row", 1)
    for d in far:
        blocks[d ^ 1] = exchange(blocks[d], "row", 1)
    near = pack_near(degrees, features, grad_out)
    nears = [near] + [exchange(near, "col", 2 * h) for h in range(1, n_part)]

    (dense,) = unpack(both, place, tiles, [], panel, group)
    late = far[-1] ^ 1
    early = {d: blocks[d] for d in range(n_row) if d != late}
    (total,) = forward(place, dense, both, early, None, n_col)
    mine, other = forward(place, dense, both, {late: blocks[late]}, total, n_col)
    other = exchange(other, "col", 1)
    pair = (mine + other.astype(f32)).astype(bf16)
    sums = [pair] + [exchange(pair, "col", 2 * h) for h in range(1, n_part)]

    layer_out, mean, grad, up = node(sums, nears, w_self, w_neigh, bias.reshape(1, width))
    up_other = exchange(up, "col", 1)
    slices, base = weight(place, mean, grad, w_self, nears)
    top = n_row // 2
    apart = [d for d in reversed(sorted(far)) if d >= top]
    joined = tuple(d ^ 1 for d in [0] + sorted(far) if d < top)
    first = [(apart[0] ^ 1,), (apart[0],)]
    rest = [(d ^ e,) for d in apart[1:] for e in (1, 0)]
    rest += [joined] + [(d ^ 1,) for d in joined]
    if both:
        near_part, far_part = unpack(False, place, tiles, [pair], panel, group, rows)
        near_places = {d: d for d in range(n_row - 2)}
        far_places = {n_row - 2: 0, n_row - 1: 1}
        backs = backward(place, far_part, far_places, up, up_other, [slices], first, n_part)
        backs.update(backward(place, near_part, near_places, up, up_other, [], rest, n_part))
    else:
        backs = backward(place, dense, None, up, up_other, [slices], first + rest, n_part)

    pairs = {}
    for d in apart:
        came = exchange(backs[(d ^ 1,)], "row", 1)
        pairs[d] = backs[(d,)].astype(f32) + came.astype(f32)
    near_came = exchange(backs[joined], "row", 1)
    for index, d in enumerate(joined):
        came = near_came[index * rows : (index + 1) * rows].astype(f32)
        pairs[d ^ 1] = backs[(d ^ 1,)].astype(f32) + came
    for d in apart:
        if d > top:
            came = exchange(pairs[d].astype(bf16), "row", d ^ top)
            pairs[top] = pairs[top] + came.astype(f32)
    total = base + pairs[0]
    for d in sorted(far):
        if d <= top:
            total = total + exchange(pairs[d].astype(bf16), "row", d).astype(f32)
    grad_in = total.astype(bf16)

    came = exchange(slices, "row", 1)
    sums = slices.astype(f32) + came.astype(f32)
    core = lax.rem(col, 2) == 0
    keep = jnp.where(core, sums[0], sums[1])
    send = jnp.where(core, sums[1], sums[0]).astype(bf16)
    grads = keep + exchange(send, "col", 1).astype(f32)
    distance = n_row // 2
    while distance > 1:
        rounded = grads.astype(bf16)
        came = exchange(rounded, "row", distance)
        grads = rounded.astype(f32) + came.astype(f32)
        distance //= 2
    mine = [grads] + [exchange(grads, "col", 2 * h) for h in range(1, n_part)]
    others = [exchange(value, "col", 1) for value in mine]
    scale = 1.0 / math.sqrt(panel * n_col)
    grad_self, grad_neigh = join(place, mine, others, scale)
    return layer_out, grad_in, grad_self, grad_neigh


def solution(mesh):
    placed = (
        P(("row", "col"), None),
        P(("row", "col"), None),
        P(("row", "col")),
        P(),
        P(),
        P(),
        P("row", "col", None),
        P("row", "col"),
        P("row", "col", None, None, None),
    )
    return jax.shard_map(
        layer,
        mesh=mesh,
        in_specs=placed,
        out_specs=(P(("row", "col"), None), P(("row", "col"), None), P(), P()),
        check_vma=False,
    )
```

```python
import functools
import math

import jax
import jax.numpy as jnp
from jax import lax
from jax.experimental import pallas as pl
from jax.experimental.pallas import tpu as pltpu
from jax.sharding import PartitionSpec as P


BOTH_FORMS_BYTES = 8 * 1024 * 1024
DIGIT_ROWS = 16

VMEM = pl.BlockSpec(memory_space=pltpu.VMEM)
HBM = pl.BlockSpec(memory_space=pltpu.HBM)
ANY = pl.BlockSpec(memory_space=pl.ANY)
SMEM = pl.BlockSpec(memory_space=pltpu.SMEM)

f32 = jnp.float32
bf16 = jnp.bfloat16


def mm(a, b):
    return jnp.dot(a, b, preferred_element_type=f32)


def mm_nt(a, b):
    return lax.dot_general(a, b, (((1,), (1,)), ((), ())), preferred_element_type=f32)


def mm_tn(a, b):
    return lax.dot_general(a, b, (((0,), (0,)), ((), ())), preferred_element_type=f32)


def params(*arrays):
    held = sum(math.prod(array.shape) * jnp.dtype(array.dtype).itemsize for array in arrays)
    return pltpu.CompilerParams(vmem_limit_bytes=held + held // 8 + (4 << 20))


def in_hbm(array):
    return pltpu.with_memory_space_constraint(array, pltpu.HBM)


def cost(nanoseconds):
    return pl.CostEstimate(flops=nanoseconds * 10**6, bytes_accessed=0, transcendentals=0)


def span(index, size):
    return pl.ds(pl.multiple_of(index * size, size), size)


def unpack_kernel(block_rows, gather, split, place_ref, count_ref, slots_hbm, masks_hbm, *refs):
    if split:
        last_ref, refs = refs[-5], refs[:-5] + refs[-4:]
    dense_ref, slots_ref, masks_ref, slots_sem, masks_sem = refs[-5:]
    slots_copy = pltpu.make_async_copy(slots_hbm, slots_ref, slots_sem)
    masks_copy = pltpu.make_async_copy(masks_hbm, masks_ref, masks_sem)
    slots_copy.start()
    masks_copy.start()
    tiles, words, width = masks_ref.shape
    height, length = dense_ref.shape
    together = math.gcd(tiles, 8)

    @pl.loop(0, height // width)
    def _(step):
        dense_ref[span(step, width), :] = jnp.zeros((width, length), bf16)

    if split:

        @pl.loop(0, last_ref.shape[0] // width)
        def _(step):
            last_ref[span(step, width), :] = jnp.zeros((width, length), bf16)

    slots_copy.wait()
    masks_copy.wait()

    def blocks(tile):
        slot = slots_ref[0, tile]
        return lax.rem(slot, block_rows), lax.div(slot, block_rows)

    if not gather:
        shifts = lax.broadcasted_iota(jnp.int32, (words, 8, width), 1)

        @pl.loop(0, count_ref[0])
        def _(tile):
            row_block, column_block = blocks(tile)
            word = jnp.broadcast_to(masks_ref[tile][:, None, :], (words, 8, width))
            bits = jnp.bitwise_and(jnp.right_shift(word, shifts), 1)
            bits = bits.astype(f32).reshape(words * 8, width).astype(bf16)
            if not split:
                dense_ref[span(column_block, width), span(row_block, width)] = bits
                return
            own, within = lax.div(column_block, split), lax.rem(column_block, split)
            spot = jnp.bitwise_xor(place_ref[0], own) * split + within
            edge = height // width

            @pl.when(spot < edge)
            def _():
                dense_ref[span(spot, width), span(row_block, width)] = bits

            @pl.when(spot >= edge)
            def _():
                last_ref[span(spot - edge, width), span(row_block, width)] = bits

        return

    places = jnp.left_shift(1, lax.broadcasted_iota(jnp.int32, (words, 8, width), 1))

    @pl.loop(0, lax.div(count_ref[0] + together - 1, together))
    def _(step):
        for t in range(together):
            tile = step * together + t
            row_block, column_block = blocks(tile)
            word = masks_ref[tile] * (tile < count_ref[0]).astype(jnp.int32)
            word = jnp.broadcast_to(word[:, None, :], (words, 8, width))
            bits = jnp.where(jnp.bitwise_and(word, places) != 0, 1.0, 0.0).astype(f32)
            bits = bits.reshape(words * 8, width).astype(bf16)
            dense_ref[span(row_block, width), span(column_block, width)] = bits.T


def unpack(gather, place, tiles, after, panel, group, rows=0):
    slot_ids, live_count, masks = tiles
    width = masks.shape[2]
    heights = [panel - 2 * rows, 2 * rows] if rows else [group if gather else panel]
    shapes = [jax.ShapeDtypeStruct((h, panel if gather else group), bf16) for h in heights]
    return pl.pallas_call(
        functools.partial(unpack_kernel, group // width, gather, rows // width),
        out_shape=shapes,
        in_specs=[SMEM, SMEM, HBM, HBM] + [ANY] * len(after),
        out_specs=[VMEM] * len(shapes),
        scratch_shapes=[
            pltpu.SMEM(slot_ids.shape, jnp.int32),
            pltpu.VMEM(masks.shape, jnp.int32),
            pltpu.SemaphoreType.DMA,
            pltpu.SemaphoreType.DMA,
        ],
        compiler_params=params(masks, *shapes),
        cost_estimate=cost(2000),
        name="unpack_gather" if gather else "unpack_spread",
    )(place, live_count, in_hbm(slot_ids), in_hbm(masks), *after)


def near_kernel(degrees_hbm, features_hbm, cotangents_hbm, near_ref, degrees_ref, sems):
    rows = features_hbm.shape[0]
    copies = [
        pltpu.make_async_copy(degrees_hbm, degrees_ref, sems.at[0]),
        pltpu.make_async_copy(features_hbm, near_ref.at[pl.ds(0, rows), :], sems.at[1]),
        pltpu.make_async_copy(cotangents_hbm, near_ref.at[pl.ds(rows, rows), :], sems.at[2]),
    ]
    for copy in copies:
        copy.start()
    copies[0].wait()
    degree = jnp.broadcast_to(degrees_ref[...], (DIGIT_ROWS, rows))
    place = lax.broadcasted_iota(jnp.int32, degree.shape, 0)
    digit = jnp.bitwise_and(jnp.right_shift(degree, 8 * jnp.minimum(place, 3)), 255)
    near_ref[pl.ds(2 * rows, DIGIT_ROWS), :] = digit.astype(f32).astype(bf16)
    copies[1].wait()
    copies[2].wait()


def pack_near(degrees, features, cotangents):
    rows, width = features.shape
    near = jax.ShapeDtypeStruct((2 * rows + DIGIT_ROWS, width), bf16)
    return pl.pallas_call(
        near_kernel,
        out_shape=near,
        in_specs=[HBM] * 3,
        out_specs=VMEM,
        scratch_shapes=[pltpu.VMEM((1, rows), jnp.int32), pltpu.SemaphoreType.DMA((3,))],
        compiler_params=params(near, near),
        cost_estimate=cost(500),
        name="near",
    )(in_hbm(degrees.reshape(1, rows)), in_hbm(features), in_hbm(cotangents))


def forward_kernel(distances, n_col, natural, last, place_ref, adjacency_ref, *refs):
    blocks, refs = refs[: len(distances)], refs[len(distances) :]
    rows = blocks[0].shape[0]
    row, col = place_ref[0], place_ref[1]
    for e in list(range(1, n_col, 2)) + list(range(0, n_col, 2)):
        own = span(jnp.bitwise_xor(col, e), rows)
        total = refs[0][pl.ds(e * rows, rows), :] if last else None
        for d, block in zip(distances, blocks):
            panel = span(jnp.bitwise_xor(row, d), rows)
            if natural:
                term = mm(adjacency_ref[own, panel], block[...])
            else:
                term = mm_tn(adjacency_ref[panel, own], block[...])
            total = term if total is None else total + term
        if last:
            out = refs[1 + e % 2]
            out[pl.ds((e // 2) * rows, rows), :] = total.astype(out.dtype)
        else:
            refs[0][pl.ds(e * rows, rows), :] = total


def forward(place, adjacency, natural, blocks, total, n_col):
    distances, arrays = list(blocks), list(blocks.values())
    rows, width = arrays[0].shape
    last = total is not None
    if last:
        half = rows * n_col // 2
        shapes = [jax.ShapeDtypeStruct((half, width), kind) for kind in (f32, bf16)]
    else:
        shapes = [jax.ShapeDtypeStruct((rows * n_col, width), f32)]
    inputs = arrays + ([total] if last else [])
    return pl.pallas_call(
        functools.partial(forward_kernel, distances, n_col, natural, last),
        out_shape=shapes,
        in_specs=[SMEM] + [VMEM] * (1 + len(inputs)),
        out_specs=[VMEM] * len(shapes),
        compiler_params=params(adjacency, *inputs, *shapes),
        cost_estimate=cost(250 * len(distances)),
        name="forward_last" if last else "forward",
    )(place, adjacency, *inputs)


def node_kernel(n_part, *refs):
    sums, refs = refs[:n_part], refs[n_part:]
    nears, refs = refs[:n_part], refs[n_part:]
    w_self, w_neigh, bias, out_ref, mean_ref, grad_ref, up_ref = refs
    rows = out_ref.shape[0]
    for h in range(n_part):
        parts = [sums[h2][pl.ds((h ^ h2) * rows, rows), :].astype(f32) for h2 in range(n_part)]
        while len(parts) > 1:
            parts = [parts[i] + parts[i + 1] for i in range(0, len(parts), 2)]
        digits = nears[h][pl.ds(2 * rows, DIGIT_ROWS), :].astype(f32)[:8, :]
        place = lax.broadcasted_iota(jnp.int32, digits.shape, 0)
        scales = jnp.where(place < 4, jnp.left_shift(1, 8 * jnp.minimum(place, 3)), 0).astype(f32)
        degree = jnp.sum((digits * scales).T, axis=1, keepdims=True)
        inverse = 1.0 / degree
        mean = (parts[0] * inverse).astype(bf16)
        preact = mm(nears[h][pl.ds(0, rows), :], w_self[...]) + mm(mean, w_neigh[...]) + bias[...]
        gate = jax.nn.sigmoid(preact)
        if h == 0:
            out_ref[...] = (preact * gate).astype(bf16)
        grad = nears[h][pl.ds(rows, rows), :].astype(f32) * gate * (1.0 + preact * (1.0 - gate))
        grad = grad.astype(bf16)
        here = pl.ds(h * rows, rows)
        mean_ref[here, :] = mean
        grad_ref[here, :] = grad
        up_ref[here, :] = (mm_nt(grad, w_neigh[...]) * inverse).astype(bf16)


def node(sums, nears, w_self, w_neigh, bias):
    n_part = len(sums)
    width = nears[0].shape[1]
    rows = sums[0].shape[0] // n_part
    all_rows = jax.ShapeDtypeStruct((rows * n_part, width), bf16)
    shapes = [jax.ShapeDtypeStruct((rows, width), bf16), all_rows, all_rows, all_rows]
    return pl.pallas_call(
        functools.partial(node_kernel, n_part),
        out_shape=shapes,
        in_specs=[VMEM] * (2 * n_part + 3),
        out_specs=[VMEM] * 4,
        compiler_params=params(*sums, *nears, w_self, w_neigh, *shapes),
        cost_estimate=cost(2000),
        name="node",
    )(*sums, *nears, w_self, w_neigh, bias)


def weight_kernel(n_part, place_ref, mean_ref, grad_ref, w_self, *refs):
    nears, (slice_ref, base_ref, total_ref) = refs[:n_part], refs[n_part:]
    rows = base_ref.shape[0]
    here = pl.ds(0, rows)
    grad_self = mm_tn(nears[0][here, :], grad_ref[here, :])
    for h in range(1, n_part):
        grad_self = grad_self + mm_tn(nears[h][here, :], grad_ref[pl.ds(h * rows, rows), :])
    grad_neigh = mm_tn(mean_ref[...], grad_ref[...])
    total_ref[0], total_ref[1] = grad_self, grad_neigh
    here = span(lax.div(place_ref[1], 2), slice_ref.shape[1])
    slice_ref[0] = total_ref[0, here, :].astype(bf16)
    slice_ref[1] = total_ref[1, here, :].astype(bf16)
    base_ref[...] = mm_nt(grad_ref[pl.ds(0, rows), :], w_self[...])


def weight(place, mean, grad, w_self, nears):
    n_part = len(nears)
    rows, width = mean.shape[0] // n_part, mean.shape[1]
    return pl.pallas_call(
        functools.partial(weight_kernel, n_part),
        out_shape=[
            jax.ShapeDtypeStruct((2, width // n_part, width), bf16),
            jax.ShapeDtypeStruct((rows, width), f32),
        ],
        in_specs=[SMEM] + [VMEM] * (3 + n_part),
        out_specs=[VMEM] * 2,
        scratch_shapes=[pltpu.VMEM((2, width, width), f32)],
        compiler_params=params(mean, grad, w_self, *nears),
        cost_estimate=cost(1300),
        name="weight",
    )(place, mean, grad, w_self, *nears)


def backward_kernel(groups, place_of, n_part, n_after, place_ref, adjacency_ref, mine_ref, other_ref, *refs):
    outs, up_ref = refs[n_after:-1], refs[-1]
    rows = mine_ref.shape[0] // n_part
    row, col = place_ref[0], place_ref[1]
    for h in range(n_part):
        here = pl.ds(h * rows, rows)
        up_ref[span(jnp.bitwise_xor(col, 2 * h), rows), :] = mine_ref[here, :]
        up_ref[span(jnp.bitwise_xor(col, 2 * h + 1), rows), :] = other_ref[here, :]
    for group, out in zip(groups, outs):
        for index, d in enumerate(group):
            if place_of is None:
                where = span(jnp.bitwise_xor(row, d), rows)
            else:
                where = pl.ds(place_of[d] * rows, rows)
            product = mm(adjacency_ref[where, :], up_ref[...])
            out[pl.ds(index * rows, rows), :] = product.astype(out.dtype)


def backward(place, adjacency, place_of, mine, other, after, groups, n_part):
    rows = mine.shape[0] // n_part
    width = mine.shape[1]
    shapes = [
        jax.ShapeDtypeStruct((len(group) * rows, width), f32 if group == (0,) else bf16)
        for group in groups
    ]
    outs = pl.pallas_call(
        functools.partial(backward_kernel, groups, place_of, n_part, len(after)),
        out_shape=shapes,
        in_specs=[SMEM] + [VMEM] * 3 + [ANY] * len(after),
        out_specs=[VMEM] * len(shapes),
        scratch_shapes=[pltpu.VMEM((2 * n_part * rows, width), bf16)],
        compiler_params=params(adjacency, mine, other, mine, other, *shapes),
        cost_estimate=cost(200 * sum(len(group) for group in groups)),
        name="backward" if (0,) in groups else "backward_far",
    )(place, adjacency, mine, other, *after)
    return dict(zip(groups, outs))


def join_kernel(n_part, scale, place_ref, *refs):
    mine, others, (self_ref, neigh_ref) = refs[:n_part], refs[n_part:-2], refs[-2:]
    first = lax.rem(place_ref[1], 2) == 0
    for h in range(n_part):
        here = span(jnp.bitwise_xor(lax.div(place_ref[1], 2), h), mine[h].shape[0])
        one, two = mine[h][...].astype(f32) * scale, others[h][...].astype(f32) * scale
        self_ref[here, :] = jnp.where(first, one, two)
        neigh_ref[here, :] = jnp.where(first, two, one)


def join(place, mine, others, scale):
    n_part = len(mine)
    width = mine[0].shape[1]
    shapes = [jax.ShapeDtypeStruct((width, width), f32)] * 2
    return pl.pallas_call(
        functools.partial(join_kernel, n_part, scale),
        out_shape=shapes,
        in_specs=[SMEM] + [VMEM] * (2 * n_part),
        out_specs=[VMEM] * 2,
        compiler_params=params(*mine, *others, *shapes),
        cost_estimate=cost(800),
        name="join",
    )(place, *mine, *others)


def exchange(value, axis, distance):
    size = lax.axis_size(axis)
    return lax.ppermute(value, axis, [(i, i ^ distance) for i in range(size)])


def layer(features, grad_out, degrees, w_self, w_neigh, bias, tile_slots, tile_count, tile_masks):
    rows, width = features.shape
    n_row, n_col = lax.axis_size("row"), lax.axis_size("col")
    n_part = n_col // 2
    row, col = lax.axis_index("row"), lax.axis_index("col")
    place = jnp.stack([row, col]).astype(jnp.int32)
    tiles = (tile_slots[0], tile_count[0], tile_masks[0, 0])
    panel, group = rows * n_row, rows * n_col
    both = 2 * panel * group * 2 <= BOTH_FORMS_BYTES

    blocks = [features] + [None] * (n_row - 1)
    far = sorted(range(2, n_row, 2), key=lambda d: (-(d & -d), d))
    for d in far:
        blocks[d] = exchange(features, "row", d)
    blocks[1] = exchange(features, "row", 1)
    for d in far:
        blocks[d ^ 1] = exchange(blocks[d], "row", 1)
    near = pack_near(degrees, features, grad_out)
    nears = [near] + [exchange(near, "col", 2 * h) for h in range(1, n_part)]

    (dense,) = unpack(both, place, tiles, [], panel, group)
    late = far[-1] ^ 1
    early = {d: blocks[d] for d in range(n_row) if d != late}
    (total,) = forward(place, dense, both, early, None, n_col)
    mine, other = forward(place, dense, both, {late: blocks[late]}, total, n_col)
    other = exchange(other, "col", 1)
    pair = (mine + other.astype(f32)).astype(bf16)
    sums = [pair] + [exchange(pair, "col", 2 * h) for h in range(1, n_part)]

    layer_out, mean, grad, up = node(sums, nears, w_self, w_neigh, bias.reshape(1, width))
    up_other = exchange(up, "col", 1)
    slices, base = weight(place, mean, grad, w_self, nears)
    top = n_row // 2
    apart = [d for d in reversed(sorted(far)) if d >= top]
    joined = tuple(d ^ 1 for d in [0] + sorted(far) if d < top)
    first = [(apart[0] ^ 1,), (apart[0],)]
    rest = [(d ^ e,) for d in apart[1:] for e in (1, 0)]
    rest += [joined] + [(d ^ 1,) for d in joined]
    if both:
        near_part, far_part = unpack(False, place, tiles, [pair], panel, group, rows)
        near_places = {d: d for d in range(n_row - 2)}
        far_places = {n_row - 2: 0, n_row - 1: 1}
        backs = backward(place, far_part, far_places, up, up_other, [slices], first, n_part)
        backs.update(backward(place, near_part, near_places, up, up_other, [], rest, n_part))
    else:
        backs = backward(place, dense, None, up, up_other, [slices], first + rest, n_part)

    pairs = {}
    for d in apart:
        came = exchange(backs[(d ^ 1,)], "row", 1)
        pairs[d] = backs[(d,)].astype(f32) + came.astype(f32)
    near_came = exchange(backs[joined], "row", 1)
    for index, d in enumerate(joined):
        came = near_came[index * rows : (index + 1) * rows].astype(f32)
        pairs[d ^ 1] = backs[(d ^ 1,)].astype(f32) + came
    for d in apart:
        if d > top:
            came = exchange(pairs[d].astype(bf16), "row", d ^ top)
            pairs[top] = pairs[top] + came.astype(f32)
    total = base + pairs[0]
    for d in sorted(far):
        if d <= top:
            total = total + exchange(pairs[d].astype(bf16), "row", d).astype(f32)
    grad_in = total.astype(bf16)

    came = exchange(slices, "row", 1)
    sums = slices.astype(f32) + came.astype(f32)
    core = lax.rem(col, 2) == 0
    keep = jnp.where(core, sums[0], sums[1])
    send = jnp.where(core, sums[1], sums[0]).astype(bf16)
    grads = keep + exchange(send, "col", 1).astype(f32)
    rounded = grads.astype(bf16)
    distance = n_row // 2
    while distance > 1:
        came = exchange(rounded, "row", distance)
        rounded = (rounded.astype(f32) + came.astype(f32)).astype(bf16)
        distance //= 2
    grads = rounded
    mine = [grads] + [exchange(grads, "col", 2 * h) for h in range(1, n_part)]
    others = [exchange(value, "col", 1) for value in mine]
    scale = 1.0 / math.sqrt(panel * n_col)
    grad_self, grad_neigh = join(place, mine, others, scale)
    return layer_out, grad_in, grad_self, grad_neigh


def solution(mesh):
    placed = (
        P(("row", "col"), None),
        P(("row", "col"), None),
        P(("row", "col")),
        P(),
        P(),
        P(),
        P("row", "col", None),
        P("row", "col"),
        P("row", "col", None, None, None),
    )
    return jax.shard_map(
        layer,
        mesh=mesh,
        in_specs=placed,
        out_specs=(P(("row", "col"), None), P(("row", "col"), None), P(), P()),
        check_vma=False,
    )
```

```python
import functools
import math

import jax
import jax.numpy as jnp
from jax import lax
from jax.experimental import pallas as pl
from jax.experimental.pallas import tpu as pltpu
from jax.sharding import PartitionSpec as P


BOTH_FORMS_BYTES = 8 * 1024 * 1024
DIGIT_ROWS = 16

VMEM = pl.BlockSpec(memory_space=pltpu.VMEM)
HBM = pl.BlockSpec(memory_space=pltpu.HBM)
ANY = pl.BlockSpec(memory_space=pl.ANY)
SMEM = pl.BlockSpec(memory_space=pltpu.SMEM)

f32 = jnp.float32
bf16 = jnp.bfloat16


def mm(a, b):
    return jnp.dot(a, b, preferred_element_type=f32)


def mm_nt(a, b):
    return lax.dot_general(a, b, (((1,), (1,)), ((), ())), preferred_element_type=f32)


def mm_tn(a, b):
    return lax.dot_general(a, b, (((0,), (0,)), ((), ())), preferred_element_type=f32)


def params(*arrays):
    held = sum(math.prod(array.shape) * jnp.dtype(array.dtype).itemsize for array in arrays)
    return pltpu.CompilerParams(vmem_limit_bytes=held + held // 8 + (4 << 20))


def in_hbm(array):
    return pltpu.with_memory_space_constraint(array, pltpu.HBM)


def cost(nanoseconds):
    return pl.CostEstimate(flops=nanoseconds * 10**6, bytes_accessed=0, transcendentals=0)


def span(index, size):
    return pl.ds(pl.multiple_of(index * size, size), size)


def unpack_kernel(block_rows, gather, split, place_ref, count_ref, slots_hbm, masks_hbm, *refs):
    if split:
        last_ref, refs = refs[-5], refs[:-5] + refs[-4:]
    dense_ref, slots_ref, masks_ref, slots_sem, masks_sem = refs[-5:]
    slots_copy = pltpu.make_async_copy(slots_hbm, slots_ref, slots_sem)
    masks_copy = pltpu.make_async_copy(masks_hbm, masks_ref, masks_sem)
    slots_copy.start()
    masks_copy.start()
    tiles, words, width = masks_ref.shape
    height, length = dense_ref.shape
    together = math.gcd(tiles, 8)

    @pl.loop(0, height // width)
    def _(step):
        dense_ref[span(step, width), :] = jnp.zeros((width, length), bf16)

    if split:

        @pl.loop(0, last_ref.shape[0] // width)
        def _(step):
            last_ref[span(step, width), :] = jnp.zeros((width, length), bf16)

    slots_copy.wait()
    masks_copy.wait()

    def blocks(tile):
        slot = slots_ref[0, tile]
        return lax.rem(slot, block_rows), lax.div(slot, block_rows)

    if not gather:
        shifts = lax.broadcasted_iota(jnp.int32, (words, 8, width), 1)

        @pl.loop(0, count_ref[0])
        def _(tile):
            row_block, column_block = blocks(tile)
            word = jnp.broadcast_to(masks_ref[tile][:, None, :], (words, 8, width))
            bits = jnp.bitwise_and(jnp.right_shift(word, shifts), 1)
            bits = bits.astype(f32).reshape(words * 8, width).astype(bf16)
            if not split:
                dense_ref[span(column_block, width), span(row_block, width)] = bits
                return
            own, within = lax.div(column_block, split), lax.rem(column_block, split)
            spot = jnp.bitwise_xor(place_ref[0], own) * split + within
            edge = height // width

            @pl.when(spot < edge)
            def _():
                dense_ref[span(spot, width), span(row_block, width)] = bits

            @pl.when(spot >= edge)
            def _():
                last_ref[span(spot - edge, width), span(row_block, width)] = bits

        return

    places = jnp.left_shift(1, lax.broadcasted_iota(jnp.int32, (words, 8, width), 1))

    @pl.loop(0, lax.div(count_ref[0] + together - 1, together))
    def _(step):
        for t in range(together):
            tile = step * together + t
            row_block, column_block = blocks(tile)
            word = masks_ref[tile] * (tile < count_ref[0]).astype(jnp.int32)
            word = jnp.broadcast_to(word[:, None, :], (words, 8, width))
            bits = jnp.where(jnp.bitwise_and(word, places) != 0, 1.0, 0.0).astype(f32)
            bits = bits.reshape(words * 8, width).astype(bf16)
            dense_ref[span(row_block, width), span(column_block, width)] = bits.T


def unpack(gather, place, tiles, after, panel, group, rows=0):
    slot_ids, live_count, masks = tiles
    width = masks.shape[2]
    heights = [panel - rows, rows] if rows else [group if gather else panel]
    shapes = [jax.ShapeDtypeStruct((h, panel if gather else group), bf16) for h in heights]
    return pl.pallas_call(
        functools.partial(unpack_kernel, group // width, gather, rows // width),
        out_shape=shapes,
        in_specs=[SMEM, SMEM, HBM, HBM] + [ANY] * len(after),
        out_specs=[VMEM] * len(shapes),
        scratch_shapes=[
            pltpu.SMEM(slot_ids.shape, jnp.int32),
            pltpu.VMEM(masks.shape, jnp.int32),
            pltpu.SemaphoreType.DMA,
            pltpu.SemaphoreType.DMA,
        ],
        compiler_params=params(masks, *shapes),
        cost_estimate=cost(2000),
        name="unpack_gather" if gather else "unpack_spread",
    )(place, live_count, in_hbm(slot_ids), in_hbm(masks), *after)


def near_kernel(degrees_hbm, features_hbm, cotangents_hbm, near_ref, degrees_ref, sems):
    rows = features_hbm.shape[0]
    copies = [
        pltpu.make_async_copy(degrees_hbm, degrees_ref, sems.at[0]),
        pltpu.make_async_copy(features_hbm, near_ref.at[pl.ds(0, rows), :], sems.at[1]),
        pltpu.make_async_copy(cotangents_hbm, near_ref.at[pl.ds(rows, rows), :], sems.at[2]),
    ]
    for copy in copies:
        copy.start()
    copies[0].wait()
    degree = jnp.broadcast_to(degrees_ref[...], (DIGIT_ROWS, rows))
    place = lax.broadcasted_iota(jnp.int32, degree.shape, 0)
    digit = jnp.bitwise_and(jnp.right_shift(degree, 8 * jnp.minimum(place, 3)), 255)
    near_ref[pl.ds(2 * rows, DIGIT_ROWS), :] = digit.astype(f32).astype(bf16)
    copies[1].wait()
    copies[2].wait()


def pack_near(degrees, features, cotangents):
    rows, width = features.shape
    near = jax.ShapeDtypeStruct((2 * rows + DIGIT_ROWS, width), bf16)
    return pl.pallas_call(
        near_kernel,
        out_shape=near,
        in_specs=[HBM] * 3,
        out_specs=VMEM,
        scratch_shapes=[pltpu.VMEM((1, rows), jnp.int32), pltpu.SemaphoreType.DMA((3,))],
        compiler_params=params(near, near),
        cost_estimate=cost(500),
        name="near",
    )(in_hbm(degrees.reshape(1, rows)), in_hbm(features), in_hbm(cotangents))


def forward_kernel(distances, columns, natural, last, place_ref, adjacency_ref, *refs):
    blocks, refs = refs[: len(distances)], refs[len(distances) :]
    rows = blocks[0].shape[0]
    row, col = place_ref[0], place_ref[1]
    for e in columns:
        own = span(jnp.bitwise_xor(col, e), rows)
        total = refs[0][pl.ds(e * rows, rows), :] if last else None
        for d, block in zip(distances, blocks):
            panel = span(jnp.bitwise_xor(row, d), rows)
            if natural:
                term = mm(adjacency_ref[own, panel], block[...])
            else:
                term = mm_tn(adjacency_ref[panel, own], block[...])
            total = term if total is None else total + term
        if last:
            refs[1][pl.ds((e // 2) * rows, rows), :] = total.astype(refs[1].dtype)
        else:
            refs[0][pl.ds(e * rows, rows), :] = total


def forward(place, adjacency, natural, blocks, total, columns):
    distances, arrays = list(blocks), list(blocks.values())
    rows, width = arrays[0].shape
    last = total is not None
    kind = bf16 if last and columns[0] % 2 else f32
    shape = jax.ShapeDtypeStruct((rows * len(columns), width), kind)
    inputs = arrays + ([total] if last else [])
    return pl.pallas_call(
        functools.partial(forward_kernel, distances, columns, natural, last),
        out_shape=shape,
        in_specs=[SMEM] + [VMEM] * (1 + len(inputs)),
        out_specs=VMEM,
        compiler_params=params(adjacency, *inputs, shape),
        cost_estimate=cost(250 * len(distances)),
        name=("forward_other" if kind == bf16 else "forward_mine") if last else "forward",
    )(place, adjacency, *inputs)


def own_kernel(n_part, *refs):
    nears, (w_self, bias, own_ref) = refs[:n_part], refs[n_part:]
    rows = own_ref.shape[0] // n_part
    for h in range(n_part):
        product = mm(nears[h][pl.ds(0, rows), :], w_self[...])
        own_ref[pl.ds(h * rows, rows), :] = product + bias[...]


def own(nears, w_self, bias, rows):
    n_part, width = len(nears), bias.shape[1]
    shape = jax.ShapeDtypeStruct((rows * n_part, width), f32)
    return pl.pallas_call(
        functools.partial(own_kernel, n_part),
        out_shape=shape,
        in_specs=[VMEM] * (n_part + 2),
        out_specs=VMEM,
        compiler_params=params(*nears, w_self, shape),
        cost_estimate=cost(500),
        name="own",
    )(*nears, w_self, bias)


def node_kernel(n_part, *refs):
    sums, refs = refs[:n_part], refs[n_part:]
    nears, refs = refs[:n_part], refs[n_part:]
    own_ref, w_neigh, out_ref, mean_ref, grad_ref, up_ref = refs
    rows = out_ref.shape[0]
    for h in range(n_part):
        parts = [sums[h2][pl.ds((h ^ h2) * rows, rows), :].astype(f32) for h2 in range(n_part)]
        while len(parts) > 1:
            parts = [parts[i] + parts[i + 1] for i in range(0, len(parts), 2)]
        digits = nears[h][pl.ds(2 * rows, DIGIT_ROWS), :].astype(f32)[:8, :]
        place = lax.broadcasted_iota(jnp.int32, digits.shape, 0)
        scales = jnp.where(place < 4, jnp.left_shift(1, 8 * jnp.minimum(place, 3)), 0).astype(f32)
        degree = jnp.sum((digits * scales).T, axis=1, keepdims=True)
        inverse = 1.0 / degree
        mean = (parts[0] * inverse).astype(bf16)
        here = pl.ds(h * rows, rows)
        preact = own_ref[here, :] + mm(mean, w_neigh[...])
        gate = jax.nn.sigmoid(preact)
        if h == 0:
            out_ref[...] = (preact * gate).astype(bf16)
        grad = nears[h][pl.ds(rows, rows), :].astype(f32) * gate * (1.0 + preact * (1.0 - gate))
        grad = grad.astype(bf16)
        mean_ref[here, :] = mean
        grad_ref[here, :] = grad
        up_ref[here, :] = (mm_nt(grad, w_neigh[...]) * inverse).astype(bf16)


def node(sums, nears, start, w_neigh):
    n_part = len(sums)
    width = nears[0].shape[1]
    rows = sums[0].shape[0] // n_part
    all_rows = jax.ShapeDtypeStruct((rows * n_part, width), bf16)
    shapes = [jax.ShapeDtypeStruct((rows, width), bf16), all_rows, all_rows, all_rows]
    return pl.pallas_call(
        functools.partial(node_kernel, n_part),
        out_shape=shapes,
        in_specs=[VMEM] * (2 * n_part + 2),
        out_specs=[VMEM] * 4,
        compiler_params=params(*sums, *nears, start, w_neigh, *shapes),
        cost_estimate=cost(2000),
        name="node",
    )(*sums, *nears, start, w_neigh)


def weight_kernel(n_part, place_ref, mean_ref, grad_ref, w_self, *refs):
    nears, (keep_ref, send_ref, base_ref, total_ref) = refs[:n_part], refs[n_part:]
    rows = base_ref.shape[0]
    here = pl.ds(0, rows)
    grad_self = mm_tn(nears[0][here, :], grad_ref[here, :])
    for h in range(1, n_part):
        grad_self = grad_self + mm_tn(nears[h][here, :], grad_ref[pl.ds(h * rows, rows), :])
    grad_neigh = mm_tn(mean_ref[...], grad_ref[...])
    first = lax.rem(place_ref[1], 2) == 0
    total_ref[0] = jnp.where(first, grad_self, grad_neigh)
    total_ref[1] = jnp.where(first, grad_neigh, grad_self)
    here = span(lax.div(place_ref[1], 2), keep_ref.shape[0])
    keep_ref[...] = total_ref[0, here, :]
    send_ref[...] = total_ref[1, here, :].astype(bf16)
    base_ref[...] = mm_nt(grad_ref[pl.ds(0, rows), :], w_self[...])


def weight(place, mean, grad, w_self, nears):
    n_part = len(nears)
    rows, width = mean.shape[0] // n_part, mean.shape[1]
    return pl.pallas_call(
        functools.partial(weight_kernel, n_part),
        out_shape=[
            jax.ShapeDtypeStruct((width // n_part, width), f32),
            jax.ShapeDtypeStruct((width // n_part, width), bf16),
            jax.ShapeDtypeStruct((rows, width), f32),
        ],
        in_specs=[SMEM] + [VMEM] * (3 + n_part),
        out_specs=[VMEM] * 3,
        scratch_shapes=[pltpu.VMEM((2, width, width), f32)],
        compiler_params=params(mean, grad, w_self, *nears),
        cost_estimate=cost(1300),
        name="weight",
    )(place, mean, grad, w_self, *nears)


def backward_kernel(groups, place_of, n_part, n_after, place_ref, adjacency_ref, mine_ref, other_ref, *refs):
    outs, up_ref = refs[n_after:-1], refs[-1]
    rows = mine_ref.shape[0] // n_part
    row, col = place_ref[0], place_ref[1]
    for h in range(n_part):
        here = pl.ds(h * rows, rows)
        up_ref[span(jnp.bitwise_xor(col, 2 * h), rows), :] = mine_ref[here, :]
        up_ref[span(jnp.bitwise_xor(col, 2 * h + 1), rows), :] = other_ref[here, :]
    for group, out in zip(groups, outs):
        for index, d in enumerate(group):
            if place_of is None:
                where = span(jnp.bitwise_xor(row, d), rows)
            else:
                where = pl.ds(place_of[d] * rows, rows)
            product = mm(adjacency_ref[where, :], up_ref[...])
            out[pl.ds(index * rows, rows), :] = product.astype(out.dtype)


def backward(place, adjacency, place_of, mine, other, after, groups, n_part):
    rows = mine.shape[0] // n_part
    width = mine.shape[1]
    shapes = [
        jax.ShapeDtypeStruct((len(group) * rows, width), f32 if group == (0,) else bf16)
        for group in groups
    ]
    outs = pl.pallas_call(
        functools.partial(backward_kernel, groups, place_of, n_part, len(after)),
        out_shape=shapes,
        in_specs=[SMEM] + [VMEM] * 3 + [ANY] * len(after),
        out_specs=[VMEM] * len(shapes),
        scratch_shapes=[pltpu.VMEM((2 * n_part * rows, width), bf16)],
        compiler_params=params(adjacency, mine, other, mine, other, *shapes),
        cost_estimate=cost(200 * sum(len(group) for group in groups)),
        name="backward" if (0,) in groups else "backward_far",
    )(place, adjacency, mine, other, *after)
    return dict(zip(groups, outs))


def join_kernel(n_part, scale, place_ref, *refs):
    mine, others, (self_ref, neigh_ref) = refs[:n_part], refs[n_part:-2], refs[-2:]
    first = lax.rem(place_ref[1], 2) == 0
    for h in range(n_part):
        here = span(jnp.bitwise_xor(lax.div(place_ref[1], 2), h), mine[h].shape[0])
        one, two = mine[h][...].astype(f32) * scale, others[h][...].astype(f32) * scale
        self_ref[here, :] = jnp.where(first, one, two)
        neigh_ref[here, :] = jnp.where(first, two, one)


def join(place, mine, others, scale):
    n_part = len(mine)
    width = mine[0].shape[1]
    shapes = [jax.ShapeDtypeStruct((width, width), f32)] * 2
    return pl.pallas_call(
        functools.partial(join_kernel, n_part, scale),
        out_shape=shapes,
        in_specs=[SMEM] + [VMEM] * (2 * n_part),
        out_specs=[VMEM] * 2,
        compiler_params=params(*mine, *others, *shapes),
        cost_estimate=cost(800),
        name="join",
    )(place, *mine, *others)


def exchange(value, axis, distance):
    size = lax.axis_size(axis)
    return lax.ppermute(value, axis, [(i, i ^ distance) for i in range(size)])


def layer(features, grad_out, degrees, w_self, w_neigh, bias, tile_slots, tile_count, tile_masks):
    rows, width = features.shape
    n_row, n_col = lax.axis_size("row"), lax.axis_size("col")
    n_part = n_col // 2
    row, col = lax.axis_index("row"), lax.axis_index("col")
    place = jnp.stack([row, col]).astype(jnp.int32)
    tiles = (tile_slots[0], tile_count[0], tile_masks[0, 0])
    panel, group = rows * n_row, rows * n_col
    both = 2 * panel * group * 2 <= BOTH_FORMS_BYTES

    blocks = [features] + [None] * (n_row - 1)
    far = sorted(range(2, n_row, 2), key=lambda d: (-(d & -d), d))
    for d in far:
        blocks[d] = exchange(features, "row", d)
    blocks[1] = exchange(features, "row", 1)
    for d in far:
        blocks[d ^ 1] = exchange(blocks[d], "row", 1)
    near = pack_near(degrees, features, grad_out)
    nears = [near] + [exchange(near, "col", 2 * h) for h in range(1, n_part)]

    (dense,) = unpack(both, place, tiles, [], panel, group)
    late = far[-1] ^ 1
    early = {d: blocks[d] for d in range(n_row) if d != late}
    columns = list(range(n_col))
    total = forward(place, dense, both, early, None, columns)
    other = forward(place, dense, both, {late: blocks[late]}, total, columns[1::2])
    other = exchange(other, "col", 1)
    mine = forward(place, dense, both, {late: blocks[late]}, total, columns[::2])
    pair = (mine + other.astype(f32)).astype(bf16)
    sums = [pair] + [exchange(pair, "col", 2 * h) for h in range(1, n_part)]

    start = own(nears, w_self, bias.reshape(1, width), rows)
    layer_out, mean, grad, up = node(sums, nears, start, w_neigh)
    up_other = exchange(up, "col", 1)
    keep, send, base = weight(place, mean, grad, w_self, nears)
    top = n_row // 2
    apart = [d for d in reversed(sorted(far)) if d >= top]
    joined = tuple(d ^ 1 for d in [0] + sorted(far) if d < top)
    first = [(apart[0] ^ 1,)]
    rest = [(d ^ e,) for d in apart[1:] for e in (1, 0)] + [(apart[0],)]
    rest += [joined] + [(d ^ 1,) for d in joined]
    if both:
        near_part, far_part = unpack(False, place, tiles, [pair], panel, group, rows)
        near_places = {d: d for d in range(n_row - 1)}
        far_places = {n_row - 1: 0}
        backs = backward(place, far_part, far_places, up, up_other, [send], first, n_part)
        backs.update(backward(place, near_part, near_places, up, up_other, [], rest, n_part))
    else:
        backs = backward(place, dense, None, up, up_other, [send], first + rest, n_part)

    pairs = {}
    for d in apart:
        came = exchange(backs[(d ^ 1,)], "row", 1)
        pairs[d] = backs[(d,)].astype(f32) + came.astype(f32)
    near_came = exchange(backs[joined], "row", 1)
    for index, d in enumerate(joined):
        came = near_came[index * rows : (index + 1) * rows].astype(f32)
        pairs[d ^ 1] = backs[(d ^ 1,)].astype(f32) + came
    for d in apart:
        if d > top:
            came = exchange(pairs[d].astype(bf16), "row", d ^ top)
            pairs[top] = pairs[top] + came.astype(f32)
    total = base + pairs[0]
    for d in sorted(far):
        if d <= top:
            total = total + exchange(pairs[d].astype(bf16), "row", d).astype(f32)
    grad_in = total.astype(bf16)

    came = exchange(send, "col", 1)
    rounded = (keep + came.astype(f32)).astype(bf16)
    for distance in [1] + [n_row >> bit for bit in range(1, n_row.bit_length() - 1)]:
        came = exchange(rounded, "row", distance)
        rounded = (rounded.astype(f32) + came.astype(f32)).astype(bf16)
    grads = rounded
    mine = [grads] + [exchange(grads, "col", 2 * h) for h in range(1, n_part)]
    others = [exchange(value, "col", 1) for value in mine]
    scale = 1.0 / math.sqrt(panel * n_col)
    grad_self, grad_neigh = join(place, mine, others, scale)
    return layer_out, grad_in, grad_self, grad_neigh


def solution(mesh):
    placed = (
        P(("row", "col"), None),
        P(("row", "col"), None),
        P(("row", "col")),
        P(),
        P(),
        P(),
        P("row", "col", None),
        P("row", "col"),
        P("row", "col", None, None, None),
    )
    return jax.shard_map(
        layer,
        mesh=mesh,
        in_specs=placed,
        out_specs=(P(("row", "col"), None), P(("row", "col"), None), P(), P()),
        check_vma=False,
    )
```

```python
import functools
import math

import jax
import jax.numpy as jnp
from jax import lax
from jax.experimental import pallas as pl
from jax.experimental.pallas import tpu as pltpu
from jax.sharding import PartitionSpec as P


BOTH_FORMS_BYTES = 8 * 1024 * 1024
DIGIT_ROWS = 16

VMEM = pl.BlockSpec(memory_space=pltpu.VMEM)
HBM = pl.BlockSpec(memory_space=pltpu.HBM)
ANY = pl.BlockSpec(memory_space=pl.ANY)
SMEM = pl.BlockSpec(memory_space=pltpu.SMEM)

f32 = jnp.float32
bf16 = jnp.bfloat16


def mm(a, b):
    return jnp.dot(a, b, preferred_element_type=f32)


def mm_nt(a, b):
    return lax.dot_general(a, b, (((1,), (1,)), ((), ())), preferred_element_type=f32)


def mm_tn(a, b):
    return lax.dot_general(a, b, (((0,), (0,)), ((), ())), preferred_element_type=f32)


def params(*arrays):
    held = sum(math.prod(array.shape) * jnp.dtype(array.dtype).itemsize for array in arrays)
    return pltpu.CompilerParams(vmem_limit_bytes=held + held // 8 + (4 << 20))


def in_hbm(array):
    return pltpu.with_memory_space_constraint(array, pltpu.HBM)


def cost(nanoseconds):
    return pl.CostEstimate(flops=nanoseconds * 10**6, bytes_accessed=0, transcendentals=0)


def span(index, size):
    return pl.ds(pl.multiple_of(index * size, size), size)


def unpack_kernel(block_rows, gather, split, count_ref, slots_hbm, masks_hbm, *refs):
    if split:
        last_ref, refs = refs[-4], refs[:-4] + refs[-3:]
    dense_ref, slots_ref, masks_ref, sems = refs[-4:]
    copies = [
        pltpu.make_async_copy(source, target, sems.at[index])
        for index, (source, target) in enumerate(
            ((masks_hbm, masks_ref), (slots_hbm, slots_ref))
        )
    ]
    for copy in copies:
        copy.start()
    tiles, words, width = masks_ref.shape
    height, length = dense_ref.shape
    together = math.gcd(tiles, 8)

    @pl.loop(0, height // width)
    def _(step):
        dense_ref[span(step, width), :] = jnp.zeros((width, length), bf16)

    if split:

        @pl.loop(0, last_ref.shape[0] // width)
        def _(step):
            last_ref[span(step, width), :] = jnp.zeros((width, length), bf16)

    for copy in copies:
        copy.wait()

    def blocks(tile):
        slot = slots_ref[0, tile]
        return lax.rem(slot, block_rows), lax.div(slot, block_rows)

    if not gather:
        shifts = lax.broadcasted_iota(jnp.int32, (words, 8, width), 1)

        @pl.loop(0, count_ref[0])
        def _(tile):
            row_block, column_block = blocks(tile)
            word = jnp.broadcast_to(masks_ref[tile][:, None, :], (words, 8, width))
            bits = jnp.bitwise_and(jnp.right_shift(word, shifts), 1)
            bits = bits.astype(f32).reshape(words * 8, width).astype(bf16)
            if not split:
                dense_ref[span(column_block, width), span(row_block, width)] = bits
                return
            own, within = lax.div(column_block, split), lax.rem(column_block, split)
            spot = jnp.bitwise_xor(lax.axis_index("row"), own) * split + within
            edge = height // width

            @pl.when(spot < edge)
            def _():
                dense_ref[span(spot, width), span(row_block, width)] = bits

            @pl.when(spot >= edge)
            def _():
                last_ref[span(spot - edge, width), span(row_block, width)] = bits

        return

    places = jnp.left_shift(1, lax.broadcasted_iota(jnp.int32, (words, 8, width), 1))

    @pl.loop(0, lax.div(count_ref[0] + together - 1, together))
    def _(step):
        for t in range(together):
            tile = step * together + t
            row_block, column_block = blocks(tile)
            word = masks_ref[tile] * (tile < count_ref[0]).astype(jnp.int32)
            word = jnp.broadcast_to(word[:, None, :], (words, 8, width))
            bits = jnp.where(jnp.bitwise_and(word, places) != 0, 1.0, 0.0).astype(f32)
            bits = bits.reshape(words * 8, width).astype(bf16)
            dense_ref[span(row_block, width), span(column_block, width)] = bits.T


def unpack(gather, tiles, after, panel, group, rows=0):
    slot_ids, live_count, masks = tiles
    width = masks.shape[2]
    heights = [panel - rows, rows] if rows else [group if gather else panel]
    shapes = [jax.ShapeDtypeStruct((h, panel if gather else group), bf16) for h in heights]
    return pl.pallas_call(
        functools.partial(unpack_kernel, group // width, gather, rows // width),
        out_shape=shapes,
        in_specs=[SMEM, HBM, HBM] + [ANY] * len(after),
        out_specs=[VMEM] * len(shapes),
        scratch_shapes=[
            pltpu.SMEM(slot_ids.shape, jnp.int32),
            pltpu.VMEM(masks.shape, jnp.int32),
            pltpu.SemaphoreType.DMA((2,)),
        ],
        compiler_params=params(masks, *shapes),
        cost_estimate=cost(2000),
        name="unpack_gather" if gather else "unpack_spread",
    )(live_count, in_hbm(slot_ids), in_hbm(masks), *after)


def near_kernel(degrees_hbm, features_hbm, cotangents_hbm, near_ref, degrees_ref, sems):
    rows = features_hbm.shape[0]
    copies = [
        pltpu.make_async_copy(degrees_hbm, degrees_ref, sems.at[0]),
        pltpu.make_async_copy(features_hbm, near_ref.at[pl.ds(0, rows), :], sems.at[1]),
        pltpu.make_async_copy(cotangents_hbm, near_ref.at[pl.ds(rows, rows), :], sems.at[2]),
    ]
    for copy in copies:
        copy.start()
    copies[0].wait()
    degree = jnp.broadcast_to(degrees_ref[...], (DIGIT_ROWS, rows))
    place = lax.broadcasted_iota(jnp.int32, degree.shape, 0)
    digit = jnp.bitwise_and(jnp.right_shift(degree, 8 * jnp.minimum(place, 3)), 255)
    near_ref[pl.ds(2 * rows, DIGIT_ROWS), :] = digit.astype(f32).astype(bf16)
    copies[1].wait()
    copies[2].wait()


def pack_near(degrees, features, cotangents):
    rows, width = features.shape
    near = jax.ShapeDtypeStruct((2 * rows + DIGIT_ROWS, width), bf16)
    return pl.pallas_call(
        near_kernel,
        out_shape=near,
        in_specs=[HBM] * 3,
        out_specs=VMEM,
        scratch_shapes=[pltpu.VMEM((1, rows), jnp.int32), pltpu.SemaphoreType.DMA((3,))],
        compiler_params=params(near, near),
        cost_estimate=cost(500),
        name="near",
    )(in_hbm(degrees.reshape(1, rows)), in_hbm(features), in_hbm(cotangents))


def forward_kernel(distances, columns, natural, last, adjacency_ref, *refs):
    blocks, refs = refs[: len(distances)], refs[len(distances) :]
    rows = blocks[0].shape[0]
    row, col = lax.axis_index("row"), lax.axis_index("col")
    for e in columns:
        own = span(jnp.bitwise_xor(col, e), rows)
        total = refs[0][pl.ds(e * rows, rows), :] if last else None
        for d, block in zip(distances, blocks):
            panel = span(jnp.bitwise_xor(row, d), rows)
            if natural:
                term = mm(adjacency_ref[own, panel], block[...])
            else:
                term = mm_tn(adjacency_ref[panel, own], block[...])
            total = term if total is None else total + term
        if last:
            refs[1][pl.ds((e // 2) * rows, rows), :] = total.astype(refs[1].dtype)
        else:
            refs[0][pl.ds(e * rows, rows), :] = total


def forward(adjacency, natural, blocks, total, columns):
    distances, arrays = list(blocks), list(blocks.values())
    rows, width = arrays[0].shape
    last = total is not None
    kind = bf16 if last and columns[0] % 2 else f32
    shape = jax.ShapeDtypeStruct((rows * len(columns), width), kind)
    inputs = arrays + ([total] if last else [])
    return pl.pallas_call(
        functools.partial(forward_kernel, distances, columns, natural, last),
        out_shape=shape,
        in_specs=[VMEM] * (1 + len(inputs)),
        out_specs=VMEM,
        compiler_params=params(adjacency, *inputs, shape),
        cost_estimate=cost(250 * len(distances)),
        name=("forward_other" if kind == bf16 else "forward_mine") if last else "forward",
    )(adjacency, *inputs)


def own_kernel(n_part, *refs):
    nears, (w_self, bias, own_ref) = refs[:n_part], refs[n_part:]
    rows = own_ref.shape[0] // n_part
    for h in range(n_part):
        product = mm(nears[h][pl.ds(0, rows), :], w_self[...])
        own_ref[pl.ds(h * rows, rows), :] = product + bias[...]


def own(nears, w_self, bias, rows):
    n_part, width = len(nears), bias.shape[1]
    shape = jax.ShapeDtypeStruct((rows * n_part, width), f32)
    return pl.pallas_call(
        functools.partial(own_kernel, n_part),
        out_shape=shape,
        in_specs=[VMEM] * (n_part + 2),
        out_specs=VMEM,
        compiler_params=params(*nears, w_self, shape),
        cost_estimate=cost(500),
        name="own",
    )(*nears, w_self, bias)


def node_kernel(n_part, *refs):
    sums, refs = refs[:n_part], refs[n_part:]
    nears, refs = refs[:n_part], refs[n_part:]
    own_ref, w_neigh, out_ref, mean_ref, grad_ref, up_ref = refs
    rows = out_ref.shape[0]
    for h in range(n_part):
        parts = [sums[h2][pl.ds((h ^ h2) * rows, rows), :].astype(f32) for h2 in range(n_part)]
        while len(parts) > 1:
            parts = [parts[i] + parts[i + 1] for i in range(0, len(parts), 2)]
        digits = nears[h][pl.ds(2 * rows, DIGIT_ROWS), :].astype(f32)[:8, :]
        place = lax.broadcasted_iota(jnp.int32, digits.shape, 0)
        scales = jnp.where(place < 4, jnp.left_shift(1, 8 * jnp.minimum(place, 3)), 0).astype(f32)
        degree = jnp.sum((digits * scales).T, axis=1, keepdims=True)
        inverse = 1.0 / degree
        mean = (parts[0] * inverse).astype(bf16)
        here = pl.ds(h * rows, rows)
        preact = own_ref[here, :] + mm(mean, w_neigh[...])
        gate = jax.nn.sigmoid(preact)
        if h == 0:
            out_ref[...] = (preact * gate).astype(bf16)
        grad = nears[h][pl.ds(rows, rows), :].astype(f32) * gate * (1.0 + preact * (1.0 - gate))
        grad = grad.astype(bf16)
        mean_ref[here, :] = mean
        grad_ref[here, :] = grad
        up_ref[here, :] = (mm_nt(grad, w_neigh[...]) * inverse).astype(bf16)


def node(sums, nears, start, w_neigh):
    n_part = len(sums)
    width = nears[0].shape[1]
    rows = sums[0].shape[0] // n_part
    all_rows = jax.ShapeDtypeStruct((rows * n_part, width), bf16)
    shapes = [pltpu.VMEM((rows, width), bf16), all_rows, all_rows, all_rows]
    return pl.pallas_call(
        functools.partial(node_kernel, n_part),
        out_shape=shapes,
        in_specs=[VMEM] * (2 * n_part + 2),
        out_specs=[VMEM] * 4,
        compiler_params=params(*sums, *nears, start, w_neigh, *shapes),
        cost_estimate=cost(2000),
        name="node",
    )(*sums, *nears, start, w_neigh)


def weight_kernel(n_part, mean_ref, grad_ref, w_self, *refs):
    nears, (keep_ref, send_ref, base_ref, total_ref) = refs[:n_part], refs[n_part:]
    rows = base_ref.shape[0]
    here = pl.ds(0, rows)
    grad_self = mm_tn(nears[0][here, :], grad_ref[here, :])
    for h in range(1, n_part):
        grad_self = grad_self + mm_tn(nears[h][here, :], grad_ref[pl.ds(h * rows, rows), :])
    grad_neigh = mm_tn(mean_ref[...], grad_ref[...])
    first = lax.rem(lax.axis_index("col"), 2) == 0
    total_ref[0] = jnp.where(first, grad_self, grad_neigh)
    total_ref[1] = jnp.where(first, grad_neigh, grad_self)
    here = span(lax.div(lax.axis_index("col"), 2), keep_ref.shape[0])
    keep_ref[...] = total_ref[0, here, :]
    send_ref[...] = total_ref[1, here, :].astype(bf16)
    base_ref[...] = mm_nt(grad_ref[pl.ds(0, rows), :], w_self[...])


def weight(mean, grad, w_self, nears):
    n_part = len(nears)
    rows, width = mean.shape[0] // n_part, mean.shape[1]
    return pl.pallas_call(
        functools.partial(weight_kernel, n_part),
        out_shape=[
            jax.ShapeDtypeStruct((width // n_part, width), f32),
            jax.ShapeDtypeStruct((width // n_part, width), bf16),
            jax.ShapeDtypeStruct((rows, width), f32),
        ],
        in_specs=[VMEM] * (3 + n_part),
        out_specs=[VMEM] * 3,
        scratch_shapes=[pltpu.VMEM((2, width, width), f32)],
        compiler_params=params(mean, grad, w_self, *nears),
        cost_estimate=cost(1300),
        name="weight",
    )(mean, grad, w_self, *nears)


def backward_kernel(groups, place_of, n_part, n_after, adjacency_ref, mine_ref, other_ref, *refs):
    outs, up_ref = refs[n_after:-1], refs[-1]
    rows = mine_ref.shape[0] // n_part
    row, col = lax.axis_index("row"), lax.axis_index("col")
    for h in range(n_part):
        here = pl.ds(h * rows, rows)
        up_ref[span(jnp.bitwise_xor(col, 2 * h), rows), :] = mine_ref[here, :]
        up_ref[span(jnp.bitwise_xor(col, 2 * h + 1), rows), :] = other_ref[here, :]
    for group, out in zip(groups, outs):
        for index, d in enumerate(group):
            if place_of is None:
                where = span(jnp.bitwise_xor(row, d), rows)
            else:
                where = pl.ds(place_of[d] * rows, rows)
            product = mm(adjacency_ref[where, :], up_ref[...])
            out[pl.ds(index * rows, rows), :] = product.astype(out.dtype)


def backward(adjacency, place_of, mine, other, after, groups, n_part):
    rows = mine.shape[0] // n_part
    width = mine.shape[1]
    shapes = [
        jax.ShapeDtypeStruct((len(group) * rows, width), f32 if group == (0,) else bf16)
        for group in groups
    ]
    outs = pl.pallas_call(
        functools.partial(backward_kernel, groups, place_of, n_part, len(after)),
        out_shape=shapes,
        in_specs=[VMEM] * 3 + [ANY] * len(after),
        out_specs=[VMEM] * len(shapes),
        scratch_shapes=[pltpu.VMEM((2 * n_part * rows, width), bf16)],
        compiler_params=params(adjacency, mine, other, mine, other, *shapes),
        cost_estimate=cost(200 * sum(len(group) for group in groups)),
        name="backward" if (0,) in groups else "backward_far",
    )(adjacency, mine, other, *after)
    return dict(zip(groups, outs))


def join_kernel(n_part, scale, *refs):
    mine, others, (self_ref, neigh_ref) = refs[:n_part], refs[n_part:-2], refs[-2:]
    first = lax.rem(lax.axis_index("col"), 2) == 0
    for h in range(n_part):
        here = span(jnp.bitwise_xor(lax.div(lax.axis_index("col"), 2), h), mine[h].shape[0])
        one, two = mine[h][...].astype(f32) * scale, others[h][...].astype(f32) * scale
        self_ref[here, :] = jnp.where(first, one, two)
        neigh_ref[here, :] = jnp.where(first, two, one)


def join(mine, others, scale):
    n_part = len(mine)
    width = mine[0].shape[1]
    shapes = [jax.ShapeDtypeStruct((width, width), f32)] * 2
    return pl.pallas_call(
        functools.partial(join_kernel, n_part, scale),
        out_shape=shapes,
        in_specs=[VMEM] * (2 * n_part),
        out_specs=[VMEM] * 2,
        compiler_params=params(*mine, *others, *shapes),
        cost_estimate=cost(800),
        name="join",
    )(*mine, *others)


def exchange(value, axis, distance):
    size = lax.axis_size(axis)
    return lax.ppermute(value, axis, [(i, i ^ distance) for i in range(size)])


def layer(features, grad_out, degrees, w_self, w_neigh, bias, tile_slots, tile_count, tile_masks):
    rows, width = features.shape
    n_row, n_col = lax.axis_size("row"), lax.axis_size("col")
    n_part = n_col // 2
    tiles = (tile_slots[0], tile_count[0], tile_masks[0, 0])
    panel, group = rows * n_row, rows * n_col
    both = 2 * panel * group * 2 <= BOTH_FORMS_BYTES

    blocks = [features] + [None] * (n_row - 1)
    far = sorted(range(2, n_row, 2), key=lambda d: (-(d & -d), d))
    for d in far:
        blocks[d] = exchange(features, "row", d)
    blocks[1] = exchange(features, "row", 1)
    for d in far:
        blocks[d ^ 1] = exchange(blocks[d], "row", 1)
    near = pack_near(degrees, features, grad_out)
    nears = [near] + [exchange(near, "col", 2 * h) for h in range(1, n_part)]

    (dense,) = unpack(both, tiles, [], panel, group)
    late = far[-1] ^ 1
    early = {d: blocks[d] for d in range(n_row) if d != late}
    columns = list(range(n_col))
    total = forward(dense, both, early, None, columns)
    other = forward(dense, both, {late: blocks[late]}, total, columns[1::2])
    other = exchange(other, "col", 1)
    mine = forward(dense, both, {late: blocks[late]}, total, columns[::2])
    pair = (mine + other.astype(f32)).astype(bf16)
    sums = [pair] + [exchange(pair, "col", 2 * h) for h in range(1, n_part)]

    start = own(nears, w_self, bias.reshape(1, width), rows)
    layer_out, mean, grad, up = node(sums, nears, start, w_neigh)
    up_other = exchange(up, "col", 1)
    keep, send, base = weight(mean, grad, w_self, nears)
    top = n_row // 2
    apart = [d for d in reversed(sorted(far)) if d >= top]
    joined = tuple(d ^ 1 for d in [0] + sorted(far) if d < top)
    first = [(apart[0] ^ 1,)]
    rest = [(d ^ e,) for d in apart[1:] for e in (1, 0)] + [(apart[0],)]
    rest += [joined] + [(d ^ 1,) for d in joined]
    if both:
        near_part, far_part = unpack(False, tiles, [pair], panel, group, rows)
        near_places = {d: d for d in range(n_row - 1)}
        far_places = {n_row - 1: 0}
        backs = backward(far_part, far_places, up, up_other, [send], first, n_part)
        backs.update(backward(near_part, near_places, up, up_other, [], rest, n_part))
    else:
        backs = backward(dense, None, up, up_other, [send], first + rest, n_part)

    pairs = {}
    for d in apart:
        came = exchange(backs[(d ^ 1,)], "row", 1)
        pairs[d] = backs[(d,)].astype(f32) + came.astype(f32)
    near_came = exchange(backs[joined], "row", 1)
    for index, d in enumerate(joined):
        came = near_came[index * rows : (index + 1) * rows].astype(f32)
        pairs[d ^ 1] = backs[(d ^ 1,)].astype(f32) + came
    for d in apart:
        if d > top:
            came = exchange(pairs[d].astype(bf16), "row", d ^ top)
            pairs[top] = pairs[top] + came.astype(f32)
    total = base + pairs[0]
    for d in sorted(far):
        if d <= top:
            total = total + exchange(pairs[d].astype(bf16), "row", d).astype(f32)
    grad_in = total.astype(bf16)

    came = exchange(send, "col", 1)
    rounded = (keep + came.astype(f32)).astype(bf16)
    for distance in [1] + [n_row >> bit for bit in range(1, n_row.bit_length() - 1)]:
        came = exchange(rounded, "row", distance)
        rounded = (rounded.astype(f32) + came.astype(f32)).astype(bf16)
    grads = rounded
    mine = [grads] + [exchange(grads, "col", 2 * h) for h in range(1, n_part)]
    others = [exchange(value, "col", 1) for value in mine]
    scale = 1.0 / math.sqrt(panel * n_col)
    grad_self, grad_neigh = join(mine, others, scale)
    return layer_out, grad_in, grad_self, grad_neigh


def solution(mesh):
    placed = (
        P(("row", "col"), None),
        P(("row", "col"), None),
        P(("row", "col")),
        P(),
        P(),
        P(),
        P("row", "col", None),
        P("row", "col"),
        P("row", "col", None, None, None),
    )
    return jax.shard_map(
        layer,
        mesh=mesh,
        in_specs=placed,
        out_specs=(P(("row", "col"), None), P(("row", "col"), None), P(), P()),
        check_vma=False,
    )
```
